128 devices in a mesh: wide: 16 (over y, z_lo, core), narrow: 8 (over x, z_hi).
Axes of the slice: x: 4, y: 4, z: 4 (z_hi: 2, z_lo: 2; z = z_hi * 2 + z_lo), core: 2. Of those that a mesh axis runs over, the one named last changes fastest.
Arguments:
- token_ids: int32 [4096], P('narrow'), may hold values from 0 to 50431
- group_ids: int32 [8], replicated, may hold values from 0 to 1
- prefix_lengths: int32 [2], replicated, may hold values from 1 to 512, as said below
- cached_lengths: int32 [8], replicated, may hold values from 0 to 2048, as said below
- embedding: bfloat16 [50432, 4096], P('narrow', 'wide'), may hold values from -6 to 6
- ln_gains: float32 [2, 4096], replicated, may hold values from 0.1 to 1.9
- qkv_weight: bfloat16 [4096, 12288], P('narrow', 'wide'), may hold values from -0.09375 to 0.09375
- out_weight: bfloat16 [4096, 4096], P('wide', 'narrow'), may hold values from -0.125 to 0.125
- up_weight: bfloat16 [4096, 16384], P('narrow', 'wide'), may hold values from -0.09375 to 0.09375
- down_weight: bfloat16 [16384, 4096], P('wide', 'narrow'), may hold values from -0.125 to 0.125
- prefix_keys: bfloat16 [2, 512, 4096], P(None, 'narrow', 'wide'), may hold values from -480 to 480
- prefix_values: bfloat16 [2, 512, 4096], P(None, 'narrow', 'wide'), may hold values from -6 to 6
- suffix_keys: bfloat16 [8, 2048, 4096], P('narrow', None, 'wide'), may hold values from -480 to 480
- suffix_values: bfloat16 [8, 2048, 4096], P('narrow', None, 'wide'), may hold values from -6 to 6
- final_gain: float32 [4096], replicated, may hold values from 0.1 to 1.9
- head_weight: bfloat16 [4096, 50432], P(None, ('wide', 'narrow')), may hold values from -0.25 to 0.25
Outputs:
- hidden_out: bfloat16 [4096, 4096], P('narrow', 'wide')
- last_rms: float32 [8], replicated
- max_logit: float32 [8], replicated
The draws below stay inside these ranges and needn't reach their ends.
Inputs may be any that keep to these rules, and one draw needn't show every extreme that they name: `prefix_lengths`: every prefix holds at least one cached position, and some prefix holds exactly 512. `cached_lengths`: some request holds exactly 2048 cached private positions.
All inputs are finite; a program needn't handle non-finite values.
Results may differ from the reference program's by a relative error of at most 0.017.
Values may be sent and summed in bfloat16 or wider, within the bound.
A program may use at most 192 MiB of HBM per device.

```python
import math
import jax
import jax.numpy as jnp
import numpy as np
from jax import lax

D = 4096
HEADS = 32
HD = 128
ROT = 32
FF = 16384
VOCAB = 50432
STRETCH = 512
GROUPS = 2
SUFFIX = 2048
REQUESTS = 8
TOKENS = 4096
PREFIX = 512
N_WIDE = 16


def draw_prefix_lengths(key, part):
    first, second = jax.random.split(jax.random.fold_in(key, 11))
    lengths = jax.random.randint(first, (GROUPS,), 1, PREFIX + 1)
    spot = jax.random.randint(second, (), 0, GROUPS)
    return jnp.where(jnp.arange(GROUPS) == spot, PREFIX, lengths).astype(jnp.int32)


def draw_cached_lengths(key, part):
    first, second = jax.random.split(jax.random.fold_in(key, 13))
    lengths = jax.random.randint(first, (REQUESTS,), 0, SUFFIX + 1)
    spot = jax.random.randint(second, (), 0, REQUESTS)
    return jnp.where(jnp.arange(REQUESTS) == spot, SUFFIX, lengths).astype(jnp.int32)


def draw_prefix_keys(key, part):
    first = jax.random.fold_in(jax.random.fold_in(key, 17), 0)
    base = jnp.clip(jax.random.normal(first, (GROUPS, PREFIX, HEADS * HD), jnp.float32), -6.0, 6.0)
    return base.astype(jnp.bfloat16)


def draw_suffix_keys(key, part):
    first = jax.random.fold_in(jax.random.fold_in(key, 19), 0)
    base = jnp.clip(jax.random.normal(first, (REQUESTS, SUFFIX, HEADS * HD), jnp.float32), -6.0, 6.0)
    return base.astype(jnp.bfloat16)


def place_ends(entries, own_key, least, top_value):
    shape = entries.shape
    index_at = [jax.random.randint(jax.random.fold_in(own_key, axis), (), 0, shape[axis]) for axis in range(len(shape))]
    entries = entries.at[tuple(index_at)].set(least)
    longest = shape.index(max(shape))
    index_at[longest] = (index_at[longest] + 1) % shape[longest]
    return entries.at[tuple(index_at)].set(top_value)


def strengthened(entries, rng, source, target, shards_of, factor):
    owner, partner = [(jnp.arange(entries.shape[dim]) // (entries.shape[dim] // shards_of)).reshape([-1 if axis == dim else 1 for axis in range(entries.ndim)]) for dim in (source, target)]
    chosen = jax.random.permutation(rng, shards_of)[partner]
    strong = (owner == chosen) | (owner == (partner + shards_of // 2) % shards_of)
    return jnp.where(strong, factor * entries, entries)


def block_scale(stream_key, dims, cuts, low, largest):
    factor_of, own = 1.0, jax.random.fold_in(stream_key, 6)
    for dim, blocks in cuts:
        draws = jnp.exp(jax.random.uniform(jax.random.fold_in(own, dim), (blocks,), jnp.float32, low / len(cuts), largest / len(cuts)))
        factor_of = factor_of * jnp.repeat(draws, dims[dim] // blocks).reshape([-1 if axis == dim else 1 for axis in range(len(dims))])
    return factor_of


def cumulative_ranks(amount, lean):
    loads = [(1 << 20) // math.isqrt(grade ** lean) + 1 for grade in range(1, amount + 1)]
    width = 1 + sum(loads) // (1 << 30)
    return np.cumsum(np.array([max(1, weight // width) for weight in loads]))


def ranked_ids(key, dims, number_of, skew):
    grid = cumulative_ranks(number_of, skew)
    ticket = jax.random.randint(jax.random.fold_in(key, 1), dims, 0, int(grid[number_of - 1]))
    standing = jnp.searchsorted(jnp.asarray(grid, jnp.int32), ticket, side="right")
    return jax.random.permutation(jax.random.fold_in(key, 2), number_of)[standing].astype(jnp.int32)


def gaussian(rng, dims, scale, limit, shards=(), kind=jnp.bfloat16):
    drawn = scale * jax.random.normal(rng, dims, jnp.float32)
    if shards:
        drawn = drawn * block_scale(rng, dims, shards, -0.22, 0.18)
    return jnp.clip(drawn, -limit, limit).astype(kind)


def heavy_noise(stream_key, shape, scale, limit, cuts, heavy, kind=jnp.bfloat16):
    drawn = scale * jax.random.normal(stream_key, shape, jnp.float32)
    if cuts:
        drawn = drawn * block_scale(stream_key, shape, cuts, -0.22, 0.18)
    return jnp.clip(strengthened(drawn, jax.random.fold_in(stream_key, 3), *heavy), -limit, limit).astype(kind)


def setup_inputs(seed: int = 0) -> dict:
    seeds = jax.random.split(jax.random.key(seed), 17)
    token_ids = place_ends(ranked_ids(seeds[0], (TOKENS,), VOCAB, 2), jax.random.fold_in(seeds[0], 3), 0, VOCAB - 1).astype(jnp.int32)
    group_ids = place_ends(jax.random.randint(seeds[1], (REQUESTS,), 0, GROUPS), jax.random.fold_in(seeds[1], 1), 0, GROUPS - 1).astype(jnp.int32)
    prefix_lengths = draw_prefix_lengths(jax.random.fold_in(seeds[16], 71), 0)
    cached_lengths = draw_cached_lengths(jax.random.fold_in(seeds[16], 71), 0)
    embedding = gaussian(seeds[4], (VOCAB, D), 1.0, 6.0, ((0, 8), (1, 16)))
    ln_gains = jnp.clip(1.0 + 0.18 * jax.random.normal(seeds[5], (2, D), jnp.float32), 0.1, 1.9)
    qkv_weight = gaussian(seeds[6], (D, 3 * HEADS * HD), D ** -0.5, 0.09375, ((0, 8), (1, 16)))
    out_weight = heavy_noise(seeds[7], (HEADS * HD, D), (HEADS * HD) ** -0.5, 0.125, ((0, 16), (1, 8)), (0, 1, 16, 2.0))
    up_weight = gaussian(seeds[8], (D, FF), D ** -0.5, 0.09375, ((0, 8), (1, 16)))
    down_weight = heavy_noise(seeds[9], (FF, D), (FF // 4) ** -0.5, 0.125, ((0, 16), (1, 8)), (0, 1, 16, 2.0))
    prefix_keys = draw_prefix_keys(jax.random.fold_in(seeds[16], 71), 0)
    prefix_values = gaussian(seeds[11], (GROUPS, PREFIX, HEADS * HD), 1.0, 6.0, ((1, 8), (2, 16)))
    suffix_keys = draw_suffix_keys(jax.random.fold_in(seeds[16], 71), 0)
    suffix_values = gaussian(seeds[13], (REQUESTS, SUFFIX, HEADS * HD), 1.0, 6.0, ((0, 8), (2, 16)))
    final_gain = jnp.clip(1.0 + 0.18 * jax.random.normal(seeds[14], (D,), jnp.float32), 0.1, 1.9)
    head_weight = gaussian(seeds[15], (D, VOCAB), (D // 9) ** -0.5, 0.25, ((1, 128),))
    return dict(token_ids=token_ids, group_ids=group_ids, prefix_lengths=prefix_lengths, cached_lengths=cached_lengths, embedding=embedding, ln_gains=ln_gains, qkv_weight=qkv_weight, out_weight=out_weight, up_weight=up_weight, down_weight=down_weight, prefix_keys=prefix_keys, prefix_values=prefix_values, suffix_keys=suffix_keys, suffix_values=suffix_values, final_gain=final_gain, head_weight=head_weight)


NEG = -1e+30

def layer_norm(rows, gain):
    values = rows.astype(jnp.float32)
    center = values - lax.optimization_barrier(jnp.mean(values, axis=-1, keepdims=True))
    spread = lax.optimization_barrier(jnp.mean(center * center, axis=-1, keepdims=True))
    return center * lax.rsqrt(spread + 1e-05) * gain

def rotate(values, places):
    half = ROT // 2
    freqs = jnp.power(10000.0, -(jnp.arange(half).astype(jnp.float32) * 2.0 / ROT))
    angles = places[:, None] * freqs[None, :]
    cosine = jnp.concatenate([jnp.cos(angles), jnp.cos(angles)], axis=-1)[:, None, :]
    sine = jnp.concatenate([jnp.sin(angles), jnp.sin(angles)], axis=-1)[:, None, :]
    turned = values[..., :ROT]
    swapped = jnp.concatenate([-turned[..., half:], turned[..., :half]], axis=-1)
    return jnp.concatenate([turned * cosine + swapped * sine, values[..., ROT:]], axis=-1)

def reference(token_ids, group_ids, prefix_lengths, cached_lengths, embedding, ln_gains, qkv_weight, out_weight, up_weight, down_weight, prefix_keys, prefix_values, suffix_keys, suffix_values, final_gain, head_weight):
    x_rows = jnp.take(embedding, token_ids, axis=0)
    norm_attn = layer_norm(x_rows, ln_gains[0]).astype(jnp.bfloat16)
    norm_mlp = layer_norm(x_rows, ln_gains[1]).astype(jnp.bfloat16)
    qkv = jnp.dot(norm_attn, qkv_weight, preferred_element_type=jnp.float32).astype(jnp.bfloat16)
    qkv = qkv.reshape(TOKENS, HEADS, 3, HD)
    position = jnp.arange(TOKENS, dtype=jnp.int32)
    request = position // STRETCH
    places = (prefix_lengths[group_ids[request]] + cached_lengths[request] + position % STRETCH).astype(jnp.float32)
    queries = rotate(qkv[:, :, 0].astype(jnp.float32), places).astype(jnp.bfloat16)
    keys = rotate(qkv[:, :, 1].astype(jnp.float32), places).astype(jnp.bfloat16)
    values = qkv[:, :, 2]
    scale = 1.0 / math.sqrt(HD)
    high = lax.Precision.HIGHEST

    def one_request(index):
        start = index * STRETCH
        q_rows = lax.dynamic_slice_in_dim(queries, start, STRETCH, 0).astype(jnp.float32)
        k_rows = lax.dynamic_slice_in_dim(keys, start, STRETCH, 0).astype(jnp.float32)
        v_rows = lax.dynamic_slice_in_dim(values, start, STRETCH, 0).astype(jnp.float32)
        group = group_ids[index]
        pre_k = lax.dynamic_index_in_dim(prefix_keys, group, 0, keepdims=False).reshape(PREFIX, HEADS, HD)
        pre_v = lax.dynamic_index_in_dim(prefix_values, group, 0, keepdims=False).reshape(PREFIX, HEADS, HD)
        suf_k = lax.dynamic_index_in_dim(suffix_keys, index, 0, keepdims=False).reshape(SUFFIX, HEADS, HD)
        suf_v = lax.dynamic_index_in_dim(suffix_values, index, 0, keepdims=False).reshape(SUFFIX, HEADS, HD)
        far_keys = jnp.concatenate([pre_k, suf_k], axis=0).astype(jnp.float32)
        far_vals = jnp.concatenate([pre_v, suf_v], axis=0).astype(jnp.float32)
        far_ok = jnp.concatenate([jnp.arange(PREFIX, dtype=jnp.int32) < prefix_lengths[group], jnp.arange(SUFFIX, dtype=jnp.int32) < cached_lengths[index]])
        far_scores = jnp.einsum('qhd,khd->qhk', q_rows, far_keys, precision=high) * scale
        far_scores = jnp.where(far_ok[None, None, :], far_scores, NEG)
        far_max = lax.optimization_barrier(jnp.max(far_scores, axis=-1))
        far_exp = jnp.where(far_ok[None, None, :], jnp.exp(far_scores - far_max[..., None]), 0.0)
        far_total = lax.optimization_barrier(jnp.sum(far_exp, axis=-1))
        far_probs = far_exp.astype(jnp.bfloat16).astype(jnp.float32)
        far_numer = jnp.einsum('qhk,khd->qhd', far_probs, far_vals, precision=high)
        causal = jnp.arange(STRETCH)[:, None] >= jnp.arange(STRETCH)[None, :]
        near_scores = jnp.einsum('qhd,khd->qhk', q_rows, k_rows, precision=high) * scale
        near_scores = jnp.where(causal[:, None, :], near_scores, NEG)
        near_max = lax.optimization_barrier(jnp.max(near_scores, axis=-1))
        near_exp = jnp.where(causal[:, None, :], jnp.exp(near_scores - near_max[..., None]), 0.0)
        near_total = lax.optimization_barrier(jnp.sum(near_exp, axis=-1))
        near_probs = near_exp.astype(jnp.bfloat16).astype(jnp.float32)
        near_numer = jnp.einsum('qhk,khd->qhd', near_probs, v_rows, precision=high)
        top = jnp.maximum(far_max, near_max)
        far_scale = jnp.exp(far_max - top)
        near_scale = jnp.exp(near_max - top)
        numer = far_numer * far_scale[..., None] + near_numer * near_scale[..., None]
        denom = far_total * far_scale + near_total * near_scale
        return (numer / denom[..., None]).reshape(STRETCH, HEADS * HD).astype(jnp.bfloat16)
    attn = lax.map(one_request, jnp.arange(REQUESTS, dtype=jnp.int32)).reshape(TOKENS, HEADS * HD)
    up = jnp.dot(norm_mlp, up_weight, preferred_element_type=jnp.float32)
    hidden = jax.nn.gelu(up, approximate=False).astype(jnp.bfloat16)
    head_cols = HEADS * HD // N_WIDE
    unit_cols = FF // N_WIDE

    def add_block(carry, block):
        attn_part = lax.dynamic_slice_in_dim(attn, block * head_cols, head_cols, 1)
        out_part = lax.dynamic_slice_in_dim(out_weight, block * head_cols, head_cols, 0)
        hid_part = lax.dynamic_slice_in_dim(hidden, block * unit_cols, unit_cols, 1)
        down_part = lax.dynamic_slice_in_dim(down_weight, block * unit_cols, unit_cols, 0)
        term = jnp.dot(attn_part, out_part, preferred_element_type=jnp.float32) + jnp.dot(hid_part, down_part, preferred_element_type=jnp.float32)
        rounded = lax.optimization_barrier(term.astype(jnp.bfloat16))
        return (carry + rounded.astype(jnp.float32), None)
    layer_sum, unused = lax.scan(add_block, jnp.zeros((TOKENS, D), jnp.float32), jnp.arange(N_WIDE, dtype=jnp.int32))
    hidden_out = (x_rows.astype(jnp.float32) + layer_sum).astype(jnp.bfloat16)
    last_rows = hidden_out.reshape(REQUESTS, STRETCH, D)[:, STRETCH - 1, :]
    last_values = last_rows.astype(jnp.float32)
    last_rms = jnp.sqrt(lax.optimization_barrier(jnp.mean(last_values * last_values, axis=-1)))
    final_rows = layer_norm(last_rows, final_gain).astype(jnp.bfloat16)
    logits = jnp.dot(final_rows, head_weight, preferred_element_type=jnp.float32)
    max_logit = lax.optimization_barrier(jnp.max(logits, axis=-1))
    return (hidden_out, last_rms, max_logit)
```

```python
import functools
import math

import jax
import jax.numpy as jnp
from jax import lax
from jax.experimental import pallas as pl
from jax.experimental.pallas import tpu as pltpu
from jax.sharding import PartitionSpec as P

HD = 128
ROT = 32
NEG = -1e30
MESH = pl.DeviceIdType.MESH
NN = 8
NWC = 8
F32 = jnp.float32
BF16 = jnp.bfloat16
VMEM_LIMIT = 67000000


def layer_norm(rows, gain):
    values = rows.astype(F32)
    center = values - jnp.mean(values, axis=-1, keepdims=True)
    spread = jnp.mean(center * center, axis=-1, keepdims=True)
    return center * lax.rsqrt(spread + 1e-05) * gain


def pick(table, index):
    match = index[:, None] == jnp.arange(table.shape[0], dtype=jnp.int32)[None, :]
    return jnp.sum(jnp.where(match, table[None, :], 0), axis=1)


def greet(devices):
    barrier = pltpu.get_barrier_semaphore()
    for device in devices:
        pl.semaphore_signal(barrier, inc=1, device_id=device, device_id_type=MESH)
    pl.semaphore_wait(barrier, len(devices))


def others(axis, count):
    me = lax.axis_index(axis)
    return [{axis: lax.rem(me + d, count)} for d in range(1, count)]


def ids_kernel(ids_ref, out_ref, ssem, rsem, lsem):
    n = lax.axis_index("narrow")
    peers = others("narrow", NN)
    greet(peers)
    local = pltpu.make_async_copy(ids_ref, out_ref.at[n], lsem)
    local.start()
    copies = []
    for d, peer in enumerate(peers):
        copies.append(
            pltpu.make_async_remote_copy(
                src_ref=ids_ref,
                dst_ref=out_ref.at[n],
                send_sem=ssem.at[d],
                recv_sem=rsem.at[d],
                device_id=peer,
                device_id_type=MESH,
            )
        )
        copies[-1].start()
    for d, copy in enumerate(copies):
        copy.wait_send()
        copy.wait_recv()
    local.wait()


def gather_ids(token_ids):
    tile = token_ids.reshape(4, 128)
    out = pl.pallas_call(
        ids_kernel,
        out_shape=jax.ShapeDtypeStruct((NN, 4, 128), jnp.int32),
        in_specs=[pl.BlockSpec(memory_space=pltpu.VMEM)],
        out_specs=pl.BlockSpec(memory_space=pltpu.VMEM),
        scratch_shapes=[
            pltpu.SemaphoreType.DMA((NN - 1,)),
            pltpu.SemaphoreType.DMA((NN - 1,)),
            pltpu.SemaphoreType.DMA,
        ],
        compiler_params=pltpu.CompilerParams(collective_id=0, has_side_effects=True),
    )(tile)
    return out.reshape(-1)


def max_kernel(val_ref, out_ref, near, far, part, ssem, rsem):
    n = lax.axis_index("narrow")
    w = lax.axis_index("wide")
    first = others("narrow", NN)
    second = others("wide", 2 * NWC)
    greet(first + second)

    def spread(src, slots, me, peers, base):
        copies = []
        for d, peer in enumerate(peers):
            copies.append(
                pltpu.make_async_remote_copy(
                    src_ref=src,
                    dst_ref=slots.at[d],
                    send_sem=ssem.at[base + d],
                    recv_sem=rsem.at[base + d],
                    device_id=peer,
                    device_id_type=MESH,
                )
            )
            copies[-1].start()
        for copy in copies:
            copy.wait_recv()
        return copies

    sent = spread(val_ref, near, n, first, 0)
    best = val_ref[...]
    for d in range(NN - 1):
        best = jnp.maximum(best, near[d])
    part[...] = best
    sent += spread(part, far, w, second, NN - 1)
    for d in range(2 * NWC - 1):
        best = jnp.maximum(best, far[d])
    out_ref[...] = best
    for copy in sent:
        copy.wait_send()


def max_over_all(values):
    tile = jnp.broadcast_to(values[:, None], (8, 128))
    out = pl.pallas_call(
        max_kernel,
        out_shape=jax.ShapeDtypeStruct((8, 128), F32),
        in_specs=[pl.BlockSpec(memory_space=pltpu.VMEM)],
        out_specs=pl.BlockSpec(memory_space=pltpu.VMEM),
        scratch_shapes=[
            pltpu.VMEM((NN - 1, 8, 128), F32),
            pltpu.VMEM((2 * NWC - 1, 8, 128), F32),
            pltpu.VMEM((8, 128), F32),
            pltpu.SemaphoreType.DMA((22,)),
            pltpu.SemaphoreType.DMA((22,)),
        ],
        compiler_params=pltpu.CompilerParams(collective_id=2, has_side_effects=True),
    )(tile)
    return out[:, 0]


class Spread:
    def __init__(self, own, buf, base, ssem, rsem, lsem, z_first):
        self.own, self.buf, self.base, self.z_first = own, buf, base, z_first
        self.ssem, self.rsem, self.lsem = ssem, rsem, lsem
        n = lax.axis_index("narrow")
        self.n = n
        self.right, self.left = lax.rem(n + 2, NN), lax.rem(n + 6, NN)
        self.far = lax.rem(n + 4, NN)
        self.half = buf.shape[1] // 2
        self.pending = []

    def flip(self, m):
        return m + 1 - 2 * lax.rem(m, 2)

    def part(self, m, h):
        if h is None:
            return self.buf.at[m]
        return self.buf.at[m, pl.ds(h * self.half, self.half)]

    def send(self, i, m, h, dst, src=None):
        copy = pltpu.make_async_remote_copy(
            src_ref=self.part(m, h) if src is None else src,
            dst_ref=self.part(m, h),
            send_sem=self.ssem.at[self.base + i],
            recv_sem=self.rsem.at[self.base + i],
            device_id={"narrow": dst},
            device_id_type=MESH,
        )
        copy.start()
        self.pending.append(copy)

    def arrive(self, i, m, h):
        pltpu.make_async_remote_copy(
            src_ref=self.part(m, h),
            dst_ref=self.part(m, h),
            send_sem=self.ssem.at[self.base + i],
            recv_sem=self.rsem.at[self.base + i],
            device_id={"narrow": self.right},
            device_id_type=MESH,
        ).wait_recv()

    def s0(self):
        n, own = self.n, self.own
        self.local = pltpu.make_async_copy(own, self.buf.at[n], self.lsem)
        self.local.start()
        self.send(0, n, None, self.right, own)
        self.send(1, n, None, self.left, own)
        self.send(2, n, None, self.flip(n), own)

    def s1(self):
        right, left, flip = self.right, self.left, self.flip
        if self.z_first:
            z = flip(self.n)
            self.arrive(2, z, None)
            self.send(3, z, None, right)
            self.send(4, z, None, left)
        self.arrive(0, left, None)
        self.send(5, left, 0, right)
        if not self.z_first:
            self.send(3, left, None, flip(self.n))
        self.arrive(1, right, None)
        self.send(6, right, 1, left)
        if not self.z_first:
            self.send(4, right, None, flip(self.n))

    def s2(self):
        right, left, far, flip = self.right, self.left, self.far, self.flip
        if self.z_first:
            self.arrive(3, flip(left), None)
            self.send(7, flip(left), 0, right)
            self.arrive(4, flip(right), None)
            self.send(8, flip(right), 1, left)
        else:
            self.arrive(5, far, 0)
            self.send(7, far, 0, flip(self.n))
            self.arrive(6, far, 1)
            self.send(8, far, 1, flip(self.n))

    def s3(self):
        right, left, far, flip = self.right, self.left, self.far, self.flip
        if self.z_first:
            self.arrive(5, far, 0)
            self.arrive(6, far, 1)
        else:
            self.arrive(2, flip(self.n), None)
            self.arrive(3, flip(left), None)
            self.arrive(4, flip(right), None)
        self.arrive(7, flip(far), 0)
        self.arrive(8, flip(far), 1)
        self.local.wait()

    def finish(self):
        for copy in self.pending:
            copy.wait_send()


def layer_kernel(
    modes,
    rows,
    wq_in,
    wu_in,
    wd_in,
    wo_in,
    pk_in,
    pv_in,
    sk_in,
    sv_in,
    gains,
    cos_t,
    sin_a,
    sin_b,
    bias,
    out_ref,
    last_ref,
    wq,
    wu,
    wd,
    wo,
    pk,
    pv,
    sk,
    sv,
    emb,
    xs,
    na,
    nm,
    qkv,
    scores,
    probs,
    attn,
    acc,
    hid,
    sib_s,
    sib_r,
    own_s,
    rs_s,
    rs_r,
    last_n,
    last_w,
    ssem,
    rsem,
    lsem,
):
    n = lax.axis_index("narrow")
    w = lax.axis_index("wide")
    c = lax.rem(w, 2)
    wc = lax.div(w, 2)
    sibling = {"wide": w + 1 - 2 * c}
    tokens, feats = out_ref.shape
    scale = 1.0 / math.sqrt(HD)

    def remote(src, dst, i, device):
        return pltpu.make_async_remote_copy(
            src_ref=src,
            dst_ref=dst,
            send_sem=ssem.at[i],
            recv_sem=rsem.at[i],
            device_id=device,
            device_id_type=MESH,
        )

    greet(others("narrow", NN) + others("wide", 2 * NWC))

    names = ["q", "d", "o", "u"]
    spreads = {}
    for k, (name, own, buf) in enumerate(zip(names, (wq_in, wd_in, wo_in, wu_in), (wq, wd, wo, wu))):
        spreads[name] = Spread(own, buf, 9 * k, ssem, rsem, lsem.at[k], modes[name])
    at = 36
    sends = []

    emb_at = at
    at += 7
    own_rows = pltpu.make_async_copy(rows.at[pl.ds(pl.multiple_of(n * tokens, tokens), tokens)], emb.at[n], lsem.at[4])
    own_rows.start()
    for d in range(1, NN):
        m = lax.rem(n + d, NN)
        copy = remote(rows.at[pl.ds(pl.multiple_of(m * tokens, tokens), tokens)], emb.at[n], emb_at + d - 1, {"narrow": m})
        copy.start()
        sends.append(copy)
    spreads["q"].s0()
    pre_at = at
    at += 14
    local_kv = []
    for j, (src, dst) in enumerate(((pk_in, pk), (pv_in, pv))):
        local_kv.append(pltpu.make_async_copy(src.at[n], dst.at[n], lsem.at[5 + j]))
        local_kv[-1].start()
        for d in range(1, NN):
            m = lax.rem(n + d, NN)
            copy = remote(src.at[m], dst.at[n], pre_at + 7 * j + d - 1, {"narrow": m})
            copy.start()
            sends.append(copy)
    for j, (src, dst) in enumerate(((sk_in, sk), (sv_in, sv))):
        local_kv.append(pltpu.make_async_copy(src.at[0], dst, lsem.at[7 + j]))
        local_kv[-1].start()

    own_rows.wait()
    for d in range(1, NN):
        src = lax.rem(n + NN - d, NN)
        remote(emb.at[src], emb.at[src], emb_at + d - 1, sibling).wait_recv()

    @pl.loop(0, tokens // 64)
    def _(i):
        r = pl.ds(pl.multiple_of(i * 64, 64), 64)
        total = emb[0, r, :].astype(F32)
        for m in range(1, NN):
            total = total + emb[m, r, :].astype(F32)
        xs[w, r, :] = total.astype(BF16)

    wide_at = at
    at += 7
    sib_at = at
    at += 8
    for d in range(1, NWC):
        m = lax.rem(wc + d, NWC)
        copy = remote(xs.at[w], xs.at[w], wide_at + d - 1, {"wide": 2 * m + c})
        copy.start()
        sends.append(copy)
    copy = remote(xs.at[w], xs.at[w], sib_at, sibling)
    copy.start()
    sends.append(copy)
    spreads["q"].s1()
    spreads["d"].s0()
    for d in range(1, NWC):
        src = 2 * lax.rem(wc + NWC - d, NWC) + c
        remote(xs.at[src], xs.at[src], wide_at + d - 1, sibling).wait_recv()
        copy = remote(xs.at[src], xs.at[src], sib_at + d, sibling)
        copy.start()
        sends.append(copy)
    spreads["q"].s2()
    spreads["o"].s0()
    spreads["u"].s0()
    spreads["d"].s1()
    for d in range(NWC):
        src = 2 * lax.rem(wc + NWC - d, NWC) + 1 - c
        remote(xs.at[src], xs.at[src], sib_at + d, sibling).wait_recv()

    wide = 2 * NWC
    total_feats = wide * feats

    @pl.loop(0, tokens // 32)
    def _(i):
        r = pl.ds(pl.multiple_of(i * 32, 32), 32)
        total = xs[0, r, :].astype(F32)
        for m in range(1, wide):
            total = total + xs[m, r, :].astype(F32)
        mean = jnp.sum(total, axis=-1, keepdims=True) * (1.0 / total_feats)
        var = jnp.zeros_like(total)
        for m in range(wide):
            center = xs[m, r, :].astype(F32) - mean
            var = var + center * center
        inv = lax.rsqrt(jnp.sum(var, axis=-1, keepdims=True) * (1.0 / total_feats) + 1e-05)
        for m in range(wide):
            cols = slice(m * feats, (m + 1) * feats)
            normed = (xs[m, r, :].astype(F32) - mean) * inv
            na[r, cols] = (normed * gains[0:1, cols]).astype(BF16)
            nm[r, cols] = (normed * gains[1:2, cols]).astype(BF16)

    spreads["q"].s3()

    @pl.loop(0, wq.shape[2] // 256)
    def _(j):
        cols = pl.ds(pl.multiple_of(j * 256, 256), 256)
        weight = wq[:, :, cols].reshape(na.shape[1], 256)
        qkv[:, cols] = jnp.dot(na[...], weight, preferred_element_type=F32).astype(BF16)

    spreads["d"].s2()
    spreads["o"].s1()

    @pl.loop(0, 4)
    def _(i):
        r = pl.ds(pl.multiple_of(i * 128, 128), 128)
        for h in range(2):
            for t in range(2):
                cols = slice((3 * h + t) * HD, (3 * h + t + 1) * HD)
                v = qkv[r, cols].astype(F32)
                turned = v * cos_t[r, :] + pltpu.roll(v, HD - ROT // 2, 1) * sin_a[r, :] + pltpu.roll(v, ROT // 2, 1) * sin_b[r, :]
                qkv[r, cols] = turned.astype(BF16)

    for copy in local_kv:
        copy.wait()
    for j, dst in enumerate((pk, pv)):
        for d in range(1, NN):
            src = lax.rem(n + NN - d, NN)
            remote(dst.at[src], dst.at[src], pre_at + 7 * j + d - 1, sibling).wait_recv()

    pre_len = pk.shape[0] * pk.shape[1]
    suf_len = sk.shape[0]
    qc = scores.shape[0]

    def attend(h):
        hc = slice(h * HD, (h + 1) * HD)
        q_cols = slice(3 * h * HD, (3 * h + 1) * HD)
        k_cols = slice((3 * h + 1) * HD, (3 * h + 2) * HD)
        v_cols = slice((3 * h + 2) * HD, (3 * h + 3) * HD)

        @pl.loop(0, tokens // qc)
        def _(i):
            r = pl.ds(pl.multiple_of(i * qc, qc), qc)
            q = qkv[r, q_cols]

            def score(keys):
                return lax.dot_general(q, keys, (((1,), (1,)), ((), ())), preferred_element_type=F32) * scale

            keys = pk[:, :, hc].reshape(pre_len, HD)
            s = score(keys) + bias[0:1, 0:pre_len]
            scores[:, 0:pre_len] = s
            top = jnp.max(s, axis=-1, keepdims=True)
            for b in range(suf_len // 512):
                lo = pre_len + b * 512
                s = score(sk[b * 512 : (b + 1) * 512, hc]) + bias[0:1, lo : lo + 512]
                scores[:, lo : lo + 512] = s
                top = jnp.maximum(top, jnp.max(s, axis=-1, keepdims=True))
            lo = pre_len + suf_len
            s = score(qkv[:, k_cols])
            row = lax.broadcasted_iota(jnp.int32, s.shape, 0) + i * qc
            col = lax.broadcasted_iota(jnp.int32, s.shape, 1)
            s = jnp.where(row >= col, s, NEG)
            scores[:, lo : lo + tokens] = s
            top = jnp.maximum(top, jnp.max(s, axis=-1, keepdims=True))
            den = jnp.zeros((qc, 1), F32)
            for b in range(scores.shape[1] // 512):
                p = jnp.exp(scores[:, b * 512 : (b + 1) * 512] - top)
                den = den + jnp.sum(p, axis=-1, keepdims=True)
                probs[:, b * 512 : (b + 1) * 512] = p.astype(BF16)
            num = jnp.dot(probs[:, 0:pre_len], pv[:, :, hc].reshape(pre_len, HD), preferred_element_type=F32)
            num = num + jnp.dot(probs[:, pre_len:lo], sv[:, hc], preferred_element_type=F32)
            num = num + jnp.dot(probs[:, lo : lo + tokens], qkv[:, v_cols], preferred_element_type=F32)
            attn[r, hc] = (num / den).astype(BF16)

    attend(0)
    spreads["u"].s1()
    attend(1)
    spreads["o"].s2()
    spreads["u"].s2()

    def up_rows(m, fresh):
        k = pl.ds(pl.multiple_of(m * wu.shape[1], wu.shape[1]), wu.shape[1])

        @pl.loop(0, wu.shape[2] // 256)
        def _(j):
            cols = pl.ds(pl.multiple_of(j * 256, 256), 256)
            part = jnp.dot(nm[:, k], wu[m, :, cols], preferred_element_type=F32)
            if fresh:
                acc[:, cols] = part
            else:
                acc[:, cols] += part

    su = spreads["u"]
    if su.z_first:
        su.local.wait()
        early = [su.flip(n), su.right, su.left, su.flip(su.right), su.flip(su.left)]
        late = [su.far, su.flip(su.far)]
        up_rows(n, True)
        for m in early:
            up_rows(m, False)
        su.arrive(5, su.far, 0)
        su.arrive(6, su.far, 1)
        up_rows(su.far, False)
        su.arrive(7, su.flip(su.far), 0)
        su.arrive(8, su.flip(su.far), 1)
        up_rows(su.flip(su.far), False)
    else:
        su.s3()
        up_rows(0, True)
        for m in range(1, NN):
            up_rows(m, False)

    @pl.loop(0, tokens // 64)
    def _(i):
        r = pl.ds(pl.multiple_of(i * 64, 64), 64)
        u = acc[r, :]
        hid[r, :] = (0.5 * u * (1.0 + lax.erf(u * math.sqrt(0.5)))).astype(BF16)

    spreads["d"].s3()
    spreads["o"].s3()

    pair_at = at
    at += 8
    rs_at = at
    at += 8

    def pair(r):
        return remote(sib_s.at[r], sib_r.at[r], pair_at + r, sibling)

    def chip(r, m):
        return remote(rs_s.at[r], rs_r.at[wc], rs_at + r, {"wide": 2 * m + c})

    def column(r):
        return lax.rem(wc + 1 + r, NWC)

    def terms(m, side):
        cols = pl.ds(pl.multiple_of(side * feats, feats), feats)
        return jnp.dot(hid[...], wd[m, :, cols], preferred_element_type=F32) + jnp.dot(
            attn[...], wo[m, :, cols], preferred_element_type=F32
        )

    def forward(r):
        pair(r).wait_recv()
        rs_s[r] = (own_s[r].astype(F32) + sib_r[r].astype(F32)).astype(BF16)
        chip(r, column(r)).start()

    @pl.loop(0, NWC)
    def _(r):
        m = column(r)
        sib_s[r] = terms(m, 1 - c).astype(BF16)
        pair(r).start()
        own_s[r] = terms(m, c).astype(BF16)

        @pl.when(r >= 1)
        def _():
            forward(r - 1)

    last = NWC - 1
    pair(last).wait_recv()
    for r in range(last):
        src = lax.rem(wc + NWC - 1 - r, NWC)
        remote(rs_r.at[src], rs_r.at[src], rs_at + r, sibling).wait_recv()
    rs_r[wc] = jnp.zeros((tokens, feats), BF16)

    @pl.loop(0, tokens // 64)
    def _(i):
        r = pl.ds(pl.multiple_of(i * 64, 64), 64)
        total = own_s[last, r, :].astype(F32) + sib_r[last, r, :].astype(F32)
        for m in range(NWC):
            total = total + rs_r[m, r, :].astype(F32)
        out_ref[r, :] = (xs[w, r, :].astype(F32) + total).astype(BF16)

    tail = out_ref[tokens - 16 : tokens, :].astype(F32)
    last_n[n] = jnp.broadcast_to(tail[15:16, :], (8, feats))
    ln_at = at
    at += 7
    for d in range(1, NN):
        copy = remote(last_n.at[n], last_n.at[n], ln_at + d - 1, {"narrow": lax.rem(n + d, NN)})
        copy.start()
        sends.append(copy)
    for d in range(1, NN):
        src = lax.rem(n + NN - d, NN)
        remote(last_n.at[src], last_n.at[src], ln_at + d - 1, sibling).wait_recv()
    pick_row = lax.broadcasted_iota(jnp.int32, (8, feats), 0)
    eight = last_n[0]
    for m in range(1, NN):
        eight = jnp.where(pick_row == m, last_n[m], eight)
    last_w[w] = eight
    lw_at = at
    at += 15
    for d in range(1, wide):
        copy = remote(last_w.at[w], last_w.at[w], lw_at + d - 1, {"wide": lax.rem(w + d, wide)})
        copy.start()
        sends.append(copy)
    for d in range(1, wide):
        src = lax.rem(w + wide - d, wide)
        remote(last_w.at[src], last_w.at[src], lw_at + d - 1, sibling).wait_recv()
    for m in range(wide):
        last_ref[:, m * feats : (m + 1) * feats] = last_w[m]

    for copy in sends:
        copy.wait_send()
    for name in names:
        spreads[name].finish()
    for r in range(NWC):
        pair(r).wait_send()
    for r in range(last):
        chip(r, column(r)).wait_send()


def layer(rows, wq, wu, wd, wo, pk, pv, sk, sv, gains, cos_t, sin_a, sin_b, bias):
    tokens = rows.shape[0] // NN
    feats = rows.shape[1]
    dim = 2 * NWC * feats
    keys = bias.shape[1]
    qc = 256
    vm = pltpu.VMEM
    anywhere = pl.BlockSpec(memory_space=pl.ANY)
    inside = pl.BlockSpec(memory_space=pltpu.VMEM)
    modes = {"q": True, "d": True, "o": True, "u": True}
    blocks = (NWC, tokens, feats)
    return pl.pallas_call(
        functools.partial(layer_kernel, modes),
        out_shape=(
            jax.ShapeDtypeStruct((tokens, feats), BF16),
            jax.ShapeDtypeStruct((NN, dim), F32),
        ),
        in_specs=[anywhere] * 9 + [inside] * 5,
        out_specs=(inside, inside),
        scratch_shapes=[
            vm((NN,) + wq.shape, BF16),
            vm((NN,) + wu.shape, BF16),
            vm((NN,) + wd.shape, BF16),
            vm((NN,) + wo.shape, BF16),
            vm(pk.shape, BF16),
            vm(pv.shape, BF16),
            vm(sk.shape[1:], BF16),
            vm(sv.shape[1:], BF16),
            vm((NN, tokens, feats), BF16),
            vm((2 * NWC, tokens, feats), BF16),
            vm((tokens, dim), BF16),
            vm((tokens, dim), BF16),
            vm((tokens, wq.shape[1]), BF16),
            vm((qc, keys), F32),
            vm((qc, keys), BF16),
            vm((tokens, feats), BF16),
            vm((tokens, wu.shape[1]), F32),
            vm((tokens, wu.shape[1]), BF16),
            vm(blocks, BF16),
            vm(blocks, BF16),
            vm(blocks, BF16),
            vm((NWC - 1, tokens, feats), BF16),
            vm(blocks, BF16),
            vm((NN, 8, feats), F32),
            vm((2 * NWC, 8, feats), F32),
            pltpu.SemaphoreType.DMA((112,)),
            pltpu.SemaphoreType.DMA((112,)),
            pltpu.SemaphoreType.DMA((9,)),
        ],
        compiler_params=pltpu.CompilerParams(
            collective_id=1, has_side_effects=True, vmem_limit_bytes=VMEM_LIMIT
        ),
    )(rows, wq, wu, wd, wo, pk, pv, sk, sv, gains, cos_t, sin_a, sin_b, bias)


def body(
    token_ids,
    group_ids,
    prefix_lengths,
    cached_lengths,
    embedding,
    ln_gains,
    qkv_weight,
    out_weight,
    up_weight,
    down_weight,
    prefix_keys,
    prefix_values,
    suffix_keys,
    suffix_values,
    final_gain,
    head_weight,
):
    n = lax.axis_index("narrow")
    stretch = token_ids.shape[0]
    all_ids = gather_ids(token_ids)
    vocab_rows = embedding.shape[0]
    local_ids = all_ids - n * vocab_rows
    inside = (local_ids >= 0) & (local_ids < vocab_rows)
    rows = jnp.take(embedding, jnp.clip(local_ids, 0, vocab_rows - 1), axis=0)
    rows = jnp.where(inside[:, None], rows, jnp.zeros((), BF16))

    second = (group_ids == 1)[:, None, None]
    pk = jnp.where(second, prefix_keys[1][None], prefix_keys[0][None])
    pv = jnp.where(second, prefix_values[1][None], prefix_values[0][None])
    me = n[None]
    group = pick(group_ids, me)
    far = pick(prefix_lengths, group)[0]
    cached = pick(cached_lengths, me)[0]
    places = (far + cached + jnp.arange(stretch, dtype=jnp.int32)).astype(F32)
    half = ROT // 2
    freqs = jnp.power(10000.0, -(jnp.arange(half).astype(F32) * 2.0 / ROT))
    angles = places[:, None] * freqs[None, :]
    cosine, sine = jnp.cos(angles), jnp.sin(angles)
    rest = HD - ROT
    cos_t = jnp.concatenate([cosine, cosine, jnp.ones((stretch, rest), F32)], axis=1)
    sin_a = jnp.concatenate([-sine, jnp.zeros((stretch, HD - half), F32)], axis=1)
    sin_b = jnp.concatenate([jnp.zeros((stretch, half), F32), sine, jnp.zeros((stretch, rest), F32)], axis=1)
    pre = NN * prefix_keys.shape[1]
    ok = jnp.concatenate(
        [
            jnp.arange(pre, dtype=jnp.int32) < far,
            jnp.arange(suffix_keys.shape[1], dtype=jnp.int32) < cached,
            jnp.ones((stretch,), bool),
        ]
    )
    bias = jnp.broadcast_to(jnp.where(ok, 0.0, NEG).astype(F32)[None, :], (8, ok.shape[0]))

    hidden_out, last_values = layer(
        rows,
        qkv_weight,
        up_weight,
        down_weight,
        out_weight,
        pk,
        pv,
        suffix_keys,
        suffix_values,
        ln_gains,
        cos_t,
        sin_a,
        sin_b,
        bias,
    )
    last_rms = jnp.sqrt(jnp.mean(last_values * last_values, axis=-1))
    final_rows = layer_norm(last_values, final_gain).astype(BF16)
    logits = jnp.dot(final_rows, head_weight, preferred_element_type=F32)
    max_logit = max_over_all(jnp.max(logits, axis=-1))
    return (hidden_out, last_rms, max_logit)


def solution(mesh):
    return jax.shard_map(
        body,
        mesh=mesh,
        in_specs=(
            P("narrow"),
            P(),
            P(),
            P(),
            P("narrow", "wide"),
            P(),
            P("narrow", "wide"),
            P("wide", "narrow"),
            P("narrow", "wide"),
            P("wide", "narrow"),
            P(None, "narrow", "wide"),
            P(None, "narrow", "wide"),
            P("narrow", None, "wide"),
            P("narrow", None, "wide"),
            P(),
            P(None, ("wide", "narrow")),
        ),
        out_specs=(P("narrow", "wide"), P(), P()),
        check_vma=False,
    )
```

```python
import math

import jax
import jax.numpy as jnp
from jax import lax
from jax.experimental import pallas as pl
from jax.experimental.pallas import tpu as pltpu
from jax.sharding import PartitionSpec as P

HD = 128
ROT = 32
NEG = -1e30
MESH = pl.DeviceIdType.MESH
NN = 8
NWC = 8
F32 = jnp.float32
BF16 = jnp.bfloat16
VMEM_LIMIT = 67000000


def layer_norm(rows, gain):
    values = rows.astype(F32)
    center = values - jnp.mean(values, axis=-1, keepdims=True)
    spread = jnp.mean(center * center, axis=-1, keepdims=True)
    return center * lax.rsqrt(spread + 1e-05) * gain


def pick(table, index):
    match = index[:, None] == jnp.arange(table.shape[0], dtype=jnp.int32)[None, :]
    return jnp.sum(jnp.where(match, table[None, :], 0), axis=1)


def greet(devices):
    barrier = pltpu.get_barrier_semaphore()
    for device in devices:
        pl.semaphore_signal(barrier, inc=1, device_id=device, device_id_type=MESH)
    pl.semaphore_wait(barrier, len(devices))


def others(axis, count):
    me = lax.axis_index(axis)
    return [{axis: lax.rem(me + d, count)} for d in range(1, count)]


def ids_kernel(ids_ref, out_ref, ssem, rsem, lsem):
    n = lax.axis_index("narrow")
    peers = others("narrow", NN)
    greet(peers)
    local = pltpu.make_async_copy(ids_ref, out_ref.at[n], lsem)
    local.start()
    copies = []
    for d, peer in enumerate(peers):
        copies.append(
            pltpu.make_async_remote_copy(
                src_ref=ids_ref,
                dst_ref=out_ref.at[n],
                send_sem=ssem.at[d],
                recv_sem=rsem.at[d],
                device_id=peer,
                device_id_type=MESH,
            )
        )
        copies[-1].start()
    for d, copy in enumerate(copies):
        copy.wait_send()
        copy.wait_recv()
    local.wait()


def gather_ids(token_ids):
    tile = token_ids.reshape(4, 128)
    out = pl.pallas_call(
        ids_kernel,
        out_shape=jax.ShapeDtypeStruct((NN, 4, 128), jnp.int32),
        in_specs=[pl.BlockSpec(memory_space=pltpu.VMEM)],
        out_specs=pl.BlockSpec(memory_space=pltpu.VMEM),
        scratch_shapes=[
            pltpu.SemaphoreType.DMA((NN - 1,)),
            pltpu.SemaphoreType.DMA((NN - 1,)),
            pltpu.SemaphoreType.DMA,
        ],
        compiler_params=pltpu.CompilerParams(collective_id=0, has_side_effects=True),
    )(tile)
    return out.reshape(-1)


def max_kernel(val_ref, out_ref, near, far, part, ssem, rsem):
    n = lax.axis_index("narrow")
    w = lax.axis_index("wide")
    first = others("narrow", NN)
    second = others("wide", 2 * NWC)
    greet(first + second)

    def spread(src, slots, me, peers, base):
        copies = []
        for d, peer in enumerate(peers):
            copies.append(
                pltpu.make_async_remote_copy(
                    src_ref=src,
                    dst_ref=slots.at[d],
                    send_sem=ssem.at[base + d],
                    recv_sem=rsem.at[base + d],
                    device_id=peer,
                    device_id_type=MESH,
                )
            )
            copies[-1].start()
        for copy in copies:
            copy.wait_recv()
        return copies

    sent = spread(val_ref, near, n, first, 0)
    best = val_ref[...]
    for d in range(NN - 1):
        best = jnp.maximum(best, near[d])
    part[...] = best
    sent += spread(part, far, w, second, NN - 1)
    for d in range(2 * NWC - 1):
        best = jnp.maximum(best, far[d])
    out_ref[...] = best
    for copy in sent:
        copy.wait_send()


def max_over_all(values):
    tile = jnp.broadcast_to(values[:, None], (8, 128))
    out = pl.pallas_call(
        max_kernel,
        out_shape=jax.ShapeDtypeStruct((8, 128), F32),
        in_specs=[pl.BlockSpec(memory_space=pltpu.VMEM)],
        out_specs=pl.BlockSpec(memory_space=pltpu.VMEM),
        scratch_shapes=[
            pltpu.VMEM((NN - 1, 8, 128), F32),
            pltpu.VMEM((2 * NWC - 1, 8, 128), F32),
            pltpu.VMEM((8, 128), F32),
            pltpu.SemaphoreType.DMA((22,)),
            pltpu.SemaphoreType.DMA((22,)),
        ],
        compiler_params=pltpu.CompilerParams(collective_id=2, has_side_effects=True),
    )(tile)
    return out[:, 0]


class Spread:
    def __init__(self, own, buf, base, sems, place):
        self.own, self.buf, self.base = own, buf, base
        self.ssem, self.rsem, self.lsem = sems
        self.n, self.w, self.x, self.c, self.home, self.away, self.swap, self.sibling = place
        self.first = 2 * self.x + self.c
        self.arrivals = [lax.rem(self.first + NN - d, NN) for d in (2, 6, 4)]

    def copy(self, i, src, m, dst):
        return pltpu.make_async_remote_copy(
            src_ref=src,
            dst_ref=self.buf.at[m],
            send_sem=self.ssem.at[self.base + i],
            recv_sem=self.rsem.at[self.base + i],
            device_id=dst,
            device_id_type=MESH,
        )

    def fan(self, src):
        for i, d in enumerate((2, 6, 4)):
            self.copy(i, src, self.first, {"narrow": lax.rem(self.n + d, NN)}).start()
        self.copy(3, src, self.first, self.sibling).start()

    def local(self):
        return pltpu.make_async_copy(self.own, self.buf.at[self.n], self.lsem)

    def z(self):
        return self.copy(7, self.own, self.n, self.swap)

    def start_home(self):
        @pl.when(self.home)
        def _():
            self.local().start()
            self.fan(self.own)

    def start_away(self):
        @pl.when(self.away)
        def _():
            self.z().start()

    def relay(self):
        @pl.when(self.away)
        def _():
            self.copy(7, self.own, self.first, self.swap).wait_recv()
            self.fan(self.buf.at[self.first])

        @pl.when(self.home)
        def _():
            self.local().wait()

    def share(self):
        for i, m in enumerate(self.arrivals):
            self.copy(i, self.buf.at[m], m, self.sibling).wait_recv()
            self.copy(4 + i, self.buf.at[m], m, self.sibling).start()

    def others(self):
        flip = 1 - 2 * self.c
        return [self.first + flip] + [m + flip for m in self.arrivals]

    def complete(self):
        for i, m in enumerate(self.others()):
            self.copy(3 + i, self.buf.at[m], m, self.sibling).wait_recv()

    def finish(self):
        for i in range(7):
            self.copy(i, self.buf.at[self.first], self.first, self.sibling).wait_send()

        @pl.when(self.away)
        def _():
            self.z().wait_send()


def layer_kernel(
    rows,
    wq_in,
    wu_in,
    wd_in,
    wo_in,
    pk_in,
    pv_in,
    sk_in,
    sv_in,
    owner,
    gains,
    cos_t,
    sin_a,
    sin_b,
    bias,
    out_ref,
    last_ref,
    wq,
    wu,
    wd,
    wo,
    pk,
    pv,
    sk,
    sv,
    emb,
    resid,
    xs,
    na,
    nm,
    qkv,
    scores,
    probs,
    attn,
    acc,
    hid,
    ry_s,
    ry_r,
    rz_s,
    rz_r,
    last_n,
    last_w,
    ssem,
    rsem,
    lsem,
):
    n = lax.axis_index("narrow")
    w = lax.axis_index("wide")
    c = lax.rem(w, 2)
    wc = lax.div(w, 2)
    y, zl = lax.div(wc, 2), lax.rem(wc, 2)
    x, zh = lax.div(n, 2), lax.rem(n, 2)
    home, away = zh == c, zh != c
    n_flip, w_flip = n + 1 - 2 * zh, w + 1 - 2 * c
    sibling = {"wide": w_flip}
    swap = {"narrow": n_flip, "wide": w_flip}
    tokens, feats = out_ref.shape
    scale = 1.0 / math.sqrt(HD)
    wide = 2 * NWC

    def remote(src, dst, i, device, j=None):
        return pltpu.make_async_remote_copy(
            src_ref=src,
            dst_ref=dst,
            send_sem=ssem.at[i],
            recv_sem=rsem.at[i if j is None else j],
            device_id=device,
            device_id_type=MESH,
        )

    greeted = []
    for d in range(NN):
        for e in range(2):
            if d or e:
                greeted.append({"narrow": lax.rem(n + d, NN), "wide": 2 * wc + lax.rem(c + e, 2)})
    for d in range(2):
        for e in range(1, NWC):
            for f in range(2):
                greeted.append({"narrow": 2 * x + lax.rem(zh + d, 2), "wide": 2 * lax.rem(wc + e, NWC) + f})
    greet(greeted)

    place = (n, w, x, c, home, away, swap, sibling)
    names = ["q", "d", "o", "u"]
    spreads = {}
    for k, (name, own, buf) in enumerate(zip(names, (wq_in, wd_in, wo_in, wu_in), (wq, wd, wo, wu))):
        spreads[name] = Spread(own, buf, 8 * k, (ssem, rsem, lsem.at[k]), place)
    sq, sd, so, su = (spreads[name] for name in names)
    at = 32
    sends = []

    emb_at = at
    at += 7
    own_rows = pltpu.make_async_copy(rows.at[pl.ds(pl.multiple_of(n * tokens, tokens), tokens)], emb.at[n], lsem.at[4])
    own_rows.start()
    for d in range(1, NN):
        m = lax.rem(n + d, NN)
        copy = remote(rows.at[pl.ds(pl.multiple_of(m * tokens, tokens), tokens)], emb.at[n], emb_at + d - 1, {"narrow": m})
        copy.start()
        sends.append(copy)
    sq.start_home()
    sq.start_away()
    sd.start_home()

    own_rows.wait()
    for d in range(1, NN):
        src = lax.rem(n + NN - d, NN)
        remote(emb.at[src], emb.at[src], emb_at + d - 1, sibling).wait_recv()

    @pl.loop(0, tokens // 64)
    def _(i):
        r = pl.ds(pl.multiple_of(i * 64, 64), 64)
        who = owner[r, :]
        total = emb[0, r, :]
        for m in range(1, NN):
            total = jnp.where(who == m, emb[m, r, :], total)
        resid[r, :] = total

        @pl.when(home)
        def _():
            xs[w, r, :] = total

    z_at = at
    at += 4
    y_at = at
    at += 12

    def over_z(d, e):
        m = {"narrow": 2 * x + lax.rem(zh + d, 2), "wide": (2 * y + lax.rem(zl + e, 2)) * 2 + zh}
        return remote(resid, xs.at[w], z_at + 2 * d + e, m, z_at + 2 * zl + c)

    for d, e in ((0, 1), (1, 0), (1, 1)):
        over_z(d, e).start()

    @pl.when(away)
    def _():
        over_z(0, 0).start()

    sq.relay()
    sd.start_away()

    suffix_at = at
    at += 2
    suffix = ((sk_in.at[0], sk), (sv_in.at[0], sv))

    @pl.when(home)
    def _():
        for j, (src, dst) in enumerate(suffix):
            pltpu.make_async_copy(src, dst, lsem.at[5 + j]).start()

    @pl.when(away)
    def _():
        for j, (src, dst) in enumerate(suffix):
            remote(src, dst, suffix_at + j, swap).start()

    def over_y(i, d):
        block = 4 * y + i
        m = {"wide": (2 * lax.rem(y + d, 4) + zl) * 2 + c}
        return remote(xs.at[block], xs.at[block], y_at + 4 * (d - 1) + i, m)

    for i in range(4):
        block = 4 * y + i

        @pl.when(jnp.logical_not(jnp.logical_and(home, 2 * zl + c == i)))
        def _():
            remote(xs.at[block], xs.at[block], z_at + i, sibling).wait_recv()

        for d in range(1, 4):
            over_y(i, d).start()

    pre_at = at
    at += 16
    prefix = ((pk_in, pk), (pv_in, pv))

    def over_x(j, d, e):
        src, dst = prefix[j]
        px, pc = lax.rem(x + d, 4), lax.rem(c + e, 2)
        m = {"narrow": 2 * px + c, "wide": 2 * wc + pc}
        return remote(src.at[2 * px + pc], dst.at[n], pre_at + 8 * j + 2 * d + e, m, pre_at + 8 * j + 4 * zh + d)

    for j in range(2):
        for d in range(4):
            for e in range(2):
                if d or e:
                    over_x(j, d, e).start()

    @pl.when(home)
    def _():
        for j, (src, dst) in enumerate(prefix):
            pltpu.make_async_copy(src.at[n], dst.at[n], lsem.at[7 + j]).start()

    @pl.when(away)
    def _():
        for j in range(2):
            over_x(j, 0, 0).start()

    so.start_home()
    so.start_away()
    su.start_home()
    su.start_away()
    sq.share()
    sd.relay()
    for i in range(4):
        for d in range(1, 4):
            block = 4 * lax.rem(y + 4 - d, 4) + i
            remote(xs.at[block], xs.at[block], y_at + 4 * (d - 1) + i, sibling).wait_recv()

    total_feats = wide * feats

    @pl.loop(0, tokens // 32)
    def _(i):
        r = pl.ds(pl.multiple_of(i * 32, 32), 32)
        total = xs[0, r, :].astype(F32)
        for m in range(1, wide):
            total = total + xs[m, r, :].astype(F32)
        mean = jnp.sum(total, axis=-1, keepdims=True) * (1.0 / total_feats)
        var = jnp.zeros_like(total)
        for m in range(wide):
            center = xs[m, r, :].astype(F32) - mean
            var = var + center * center
        inv = lax.rsqrt(jnp.sum(var, axis=-1, keepdims=True) * (1.0 / total_feats) + 1e-05)
        for m in range(wide):
            cols = slice(m * feats, (m + 1) * feats)
            normed = (xs[m, r, :].astype(F32) - mean) * inv
            na[r, cols] = (normed * gains[0:1, cols]).astype(BF16)
            nm[r, cols] = (normed * gains[1:2, cols]).astype(BF16)

    so.relay()
    su.relay()
    sq.complete()

    @pl.loop(0, wq.shape[2] // 256)
    def _(j):
        cols = pl.ds(pl.multiple_of(j * 256, 256), 256)
        weight = wq[:, :, cols].reshape(na.shape[1], 256)
        qkv[:, cols] = jnp.dot(na[...], weight, preferred_element_type=F32).astype(BF16)

    sd.share()

    @pl.loop(0, 4)
    def _(i):
        r = pl.ds(pl.multiple_of(i * 128, 128), 128)
        for h in range(2):
            for t in range(2):
                cols = slice((3 * h + t) * HD, (3 * h + t + 1) * HD)
                v = qkv[r, cols].astype(F32)
                turned = v * cos_t[r, :] + pltpu.roll(v, HD - ROT // 2, 1) * sin_a[r, :] + pltpu.roll(v, ROT // 2, 1) * sin_b[r, :]
                qkv[r, cols] = turned.astype(BF16)

    @pl.when(home)
    def _():
        for j, (src, dst) in enumerate(suffix):
            pltpu.make_async_copy(src, dst, lsem.at[5 + j]).wait()

    @pl.when(away)
    def _():
        for j, (src, dst) in enumerate(suffix):
            remote(src, dst, suffix_at + j, swap).wait_recv()

    for j, (src, dst) in enumerate(prefix):
        for sz in range(2):
            for d in range(4):
                m = 2 * lax.rem(x + 4 - d, 4) + sz
                arrival = remote(dst.at[m], dst.at[m], pre_at, sibling, pre_at + 8 * j + 4 * sz + d)
                if d:
                    arrival.wait_recv()
                else:
                    mine = jnp.logical_and(home, zh == sz)

                    @pl.when(mine)
                    def _():
                        pltpu.make_async_copy(src.at[n], dst.at[n], lsem.at[7 + j]).wait()

                    @pl.when(jnp.logical_not(mine))
                    def _():
                        arrival.wait_recv()

    pre_len = pk.shape[0] * pk.shape[1]
    suf_len = sk.shape[0]
    qc = scores.shape[0]

    def attend(h):
        hc = slice(h * HD, (h + 1) * HD)
        q_cols = slice(3 * h * HD, (3 * h + 1) * HD)
        k_cols = slice((3 * h + 1) * HD, (3 * h + 2) * HD)
        v_cols = slice((3 * h + 2) * HD, (3 * h + 3) * HD)

        @pl.loop(0, tokens // qc)
        def _(i):
            r = pl.ds(pl.multiple_of(i * qc, qc), qc)
            q = qkv[r, q_cols]

            def score(keys):
                return lax.dot_general(q, keys, (((1,), (1,)), ((), ())), preferred_element_type=F32) * scale

            keys = pk[:, :, hc].reshape(pre_len, HD)
            s = score(keys) + bias[0:1, 0:pre_len]
            scores[:, 0:pre_len] = s
            top = jnp.max(s, axis=-1, keepdims=True)
            for b in range(suf_len // 512):
                lo = pre_len + b * 512
                s = score(sk[b * 512 : (b + 1) * 512, hc]) + bias[0:1, lo : lo + 512]
                scores[:, lo : lo + 512] = s
                top = jnp.maximum(top, jnp.max(s, axis=-1, keepdims=True))
            lo = pre_len + suf_len
            s = score(qkv[:, k_cols])
            row = lax.broadcasted_iota(jnp.int32, s.shape, 0) + i * qc
            col = lax.broadcasted_iota(jnp.int32, s.shape, 1)
            s = jnp.where(row >= col, s, NEG)
            scores[:, lo : lo + tokens] = s
            top = jnp.maximum(top, jnp.max(s, axis=-1, keepdims=True))
            den = jnp.zeros((qc, 1), F32)
            for b in range(scores.shape[1] // 512):
                p = jnp.exp(scores[:, b * 512 : (b + 1) * 512] - top)
                den = den + jnp.sum(p, axis=-1, keepdims=True)
                probs[:, b * 512 : (b + 1) * 512] = p.astype(BF16)
            num = jnp.dot(probs[:, 0:pre_len], pv[:, :, hc].reshape(pre_len, HD), preferred_element_type=F32)
            num = num + jnp.dot(probs[:, pre_len:lo], sv[:, hc], preferred_element_type=F32)
            num = num + jnp.dot(probs[:, lo : lo + tokens], qkv[:, v_cols], preferred_element_type=F32)
            attn[r, hc] = (num / den).astype(BF16)

    attend(0)
    so.share()
    su.share()
    attend(1)

    def up_rows(m, fresh):
        k = pl.ds(pl.multiple_of(m * wu.shape[1], wu.shape[1]), wu.shape[1])

        @pl.loop(0, wu.shape[2] // 256)
        def _(j):
            cols = pl.ds(pl.multiple_of(j * 256, 256), 256)
            part = jnp.dot(nm[:, k], wu[m, :, cols], preferred_element_type=F32)
            if fresh:
                acc[:, cols] = part
            else:
                acc[:, cols] += part

    up_rows(su.first, True)
    for m in su.arrivals:
        up_rows(m, False)
    su.complete()
    for m in su.others():
        up_rows(m, False)

    @pl.loop(0, tokens // 64)
    def _(i):
        r = pl.ds(pl.multiple_of(i * 64, 64), 64)
        u = acc[r, :]
        hid[r, :] = (0.5 * u * (1.0 + lax.erf(u * math.sqrt(0.5)))).astype(BF16)

    sd.complete()
    so.complete()

    sum_at = at
    at += 3
    part_at = at
    at += 4
    span = wd.shape[2]

    def terms(m):
        return jnp.dot(hid[...], wd[m], preferred_element_type=F32) + jnp.dot(
            attn[...], wo[m], preferred_element_type=F32
        )

    def to_y(r):
        m = {"wide": (2 * lax.rem(y + 1 + r, 4) + zl) * 2 + c}
        return remote(ry_s.at[r], ry_r.at[r], sum_at + r, m)

    for r in range(3):

        @pl.loop(0, 2)
        def _(j):
            cols = pl.ds(pl.multiple_of(j * span, span), span)
            ry_s[r, :, cols] = terms(2 * lax.rem(y + 1 + r, 4) + j).astype(BF16)

        to_y(r).start()

    @pl.loop(0, 2)
    def _(j):
        cols = pl.ds(pl.multiple_of(j * span, span), span)
        acc[:, cols] = terms(2 * y + j)

    for r in range(3):
        to_y(r).wait_recv()
    spot = 2 * zh + zl

    def to_z(i):
        m = {"narrow": 2 * x + c, "wide": 4 * y + i}
        return remote(rz_s.at[i], rz_r.at[spot], part_at + i, m, part_at + spot)

    for i in range(4):
        cols = slice(i * feats, (i + 1) * feats)

        @pl.loop(0, tokens // 64)
        def _(k):
            r = pl.ds(pl.multiple_of(k * 64, 64), 64)
            total = acc[r, cols]
            for m in range(3):
                total = total + ry_r[m, r, cols].astype(F32)
            rz_s[i, r, :] = total.astype(BF16)

        mine = jnp.logical_and(home, 2 * zl + c == i)

        @pl.when(jnp.logical_not(mine))
        def _():
            to_z(i).start()

        @pl.when(mine)
        def _():
            rz_r[spot] = rz_s[i]

    for i in range(4):

        @pl.when(jnp.logical_not(jnp.logical_and(home, spot == i)))
        def _():
            remote(rz_r.at[i], rz_r.at[i], part_at, sibling, part_at + i).wait_recv()

    @pl.loop(0, tokens // 64)
    def _(i):
        r = pl.ds(pl.multiple_of(i * 64, 64), 64)
        total = rz_r[0, r, :].astype(F32)
        for m in range(1, 4):
            total = total + rz_r[m, r, :].astype(F32)
        out_ref[r, :] = (resid[r, :].astype(F32) + total).astype(BF16)

    tail = out_ref[tokens - 16 : tokens, :].astype(F32)
    last_n[n] = jnp.broadcast_to(tail[15:16, :], (8, feats))
    ln_at = at
    at += 7
    for d in range(1, NN):
        copy = remote(last_n.at[n], last_n.at[n], ln_at + d - 1, {"narrow": lax.rem(n + d, NN)})
        copy.start()
        sends.append(copy)
    for d in range(1, NN):
        src = lax.rem(n + NN - d, NN)
        remote(last_n.at[src], last_n.at[src], ln_at + d - 1, sibling).wait_recv()
    pick_row = lax.broadcasted_iota(jnp.int32, (8, feats), 0)
    eight = last_n[0]
    for m in range(1, NN):
        eight = jnp.where(pick_row == m, last_n[m], eight)
    last_w[w] = eight
    lw_at = at
    at += 15
    for d in range(1, wide):
        copy = remote(last_w.at[w], last_w.at[w], lw_at + d - 1, {"wide": lax.rem(w + d, wide)})
        copy.start()
        sends.append(copy)
    for d in range(1, wide):
        src = lax.rem(w + wide - d, wide)
        remote(last_w.at[src], last_w.at[src], lw_at + d - 1, sibling).wait_recv()
    for m in range(wide):
        last_ref[:, m * feats : (m + 1) * feats] = last_w[m]

    for copy in sends:
        copy.wait_send()
    for name in names:
        spreads[name].finish()
    for d, e in ((0, 1), (1, 0), (1, 1)):
        over_z(d, e).wait_send()
    for i in range(4):
        for d in range(1, 4):
            over_y(i, d).wait_send()
    for j in range(2):
        for d in range(4):
            for e in range(2):
                if d or e:
                    over_x(j, d, e).wait_send()

    @pl.when(away)
    def _():
        over_z(0, 0).wait_send()
        for j, (src, dst) in enumerate(suffix):
            remote(src, dst, suffix_at + j, swap).wait_send()
        for j in range(2):
            over_x(j, 0, 0).wait_send()

    for r in range(3):
        to_y(r).wait_send()
    for i in range(4):

        @pl.when(jnp.logical_not(jnp.logical_and(home, 2 * zl + c == i)))
        def _():
            to_z(i).wait_send()


def layer(rows, wq, wu, wd, wo, pk, pv, sk, sv, owner, gains, cos_t, sin_a, sin_b, bias):
    tokens = rows.shape[0] // NN
    feats = rows.shape[1]
    dim = 2 * NWC * feats
    keys = bias.shape[1]
    qc = 256
    vm = pltpu.VMEM
    anywhere = pl.BlockSpec(memory_space=pl.ANY)
    inside = pl.BlockSpec(memory_space=pltpu.VMEM)
    four = (4, tokens, feats)
    groups = (3, tokens, 4 * feats)
    return pl.pallas_call(
        layer_kernel,
        out_shape=(
            jax.ShapeDtypeStruct((tokens, feats), BF16),
            jax.ShapeDtypeStruct((NN, dim), F32),
        ),
        in_specs=[anywhere] * 9 + [inside] * 6,
        out_specs=(inside, inside),
        scratch_shapes=[
            vm((NN,) + wq.shape, BF16),
            vm((NN,) + wu.shape, BF16),
            vm((NN,) + wd.shape, BF16),
            vm((NN,) + wo.shape, BF16),
            vm(pk.shape, BF16),
            vm(pv.shape, BF16),
            vm(sk.shape[1:], BF16),
            vm(sv.shape[1:], BF16),
            vm((NN, tokens, feats), BF16),
            vm((tokens, feats), BF16),
            vm((2 * NWC, tokens, feats), BF16),
            vm((tokens, dim), BF16),
            vm((tokens, dim), BF16),
            vm((tokens, wq.shape[1]), BF16),
            vm((qc, keys), F32),
            vm((qc, keys), BF16),
            vm((tokens, feats), BF16),
            vm((tokens, wu.shape[1]), F32),
            vm((tokens, wu.shape[1]), BF16),
            vm(groups, BF16),
            vm(groups, BF16),
            vm(four, BF16),
            vm(four, BF16),
            vm((NN, 8, feats), F32),
            vm((2 * NWC, 8, feats), F32),
            pltpu.SemaphoreType.DMA((112,)),
            pltpu.SemaphoreType.DMA((112,)),
            pltpu.SemaphoreType.DMA((9,)),
        ],
        compiler_params=pltpu.CompilerParams(
            collective_id=1, has_side_effects=True, vmem_limit_bytes=VMEM_LIMIT
        ),
    )(rows, wq, wu, wd, wo, pk, pv, sk, sv, owner, gains, cos_t, sin_a, sin_b, bias)


def body(
    token_ids,
    group_ids,
    prefix_lengths,
    cached_lengths,
    embedding,
    ln_gains,
    qkv_weight,
    out_weight,
    up_weight,
    down_weight,
    prefix_keys,
    prefix_values,
    suffix_keys,
    suffix_values,
    final_gain,
    head_weight,
):
    n = lax.axis_index("narrow")
    stretch = token_ids.shape[0]
    all_ids = gather_ids(token_ids)
    vocab_rows = embedding.shape[0]
    local_ids = all_ids - n * vocab_rows
    rows = jnp.take(embedding, jnp.clip(local_ids, 0, vocab_rows - 1), axis=0)
    owner = jnp.broadcast_to((token_ids // vocab_rows)[:, None], (stretch, embedding.shape[1]))

    second = (group_ids == 1)[:, None, None]
    pk = jnp.where(second, prefix_keys[1][None], prefix_keys[0][None])
    pv = jnp.where(second, prefix_values[1][None], prefix_values[0][None])
    me = (2 * (n // 2) + lax.axis_index("wide") % 2)[None]
    group = pick(group_ids, me)
    far = pick(prefix_lengths, group)[0]
    cached = pick(cached_lengths, me)[0]
    places = (far + cached + jnp.arange(stretch, dtype=jnp.int32)).astype(F32)
    half = ROT // 2
    freqs = jnp.power(10000.0, -(jnp.arange(half).astype(F32) * 2.0 / ROT))
    angles = places[:, None] * freqs[None, :]
    cosine, sine = jnp.cos(angles), jnp.sin(angles)
    rest = HD - ROT
    cos_t = jnp.concatenate([cosine, cosine, jnp.ones((stretch, rest), F32)], axis=1)
    sin_a = jnp.concatenate([-sine, jnp.zeros((stretch, HD - half), F32)], axis=1)
    sin_b = jnp.concatenate([jnp.zeros((stretch, half), F32), sine, jnp.zeros((stretch, rest), F32)], axis=1)
    pre = NN * prefix_keys.shape[1]
    ok = jnp.concatenate(
        [
            jnp.arange(pre, dtype=jnp.int32) < far,
            jnp.arange(suffix_keys.shape[1], dtype=jnp.int32) < cached,
            jnp.ones((stretch,), bool),
        ]
    )
    bias = jnp.broadcast_to(jnp.where(ok, 0.0, NEG).astype(F32)[None, :], (8, ok.shape[0]))

    hidden_out, last_values = layer(
        rows,
        qkv_weight,
        up_weight,
        down_weight,
        out_weight,
        pk,
        pv,
        suffix_keys,
        suffix_values,
        owner,
        ln_gains,
        cos_t,
        sin_a,
        sin_b,
        bias,
    )
    last_rms = jnp.sqrt(jnp.mean(last_values * last_values, axis=-1))
    final_rows = layer_norm(last_values, final_gain).astype(BF16)
    logits = jnp.dot(final_rows, head_weight, preferred_element_type=F32)
    max_logit = max_over_all(jnp.max(logits, axis=-1))
    return (hidden_out, last_rms, max_logit)


def solution(mesh):
    return jax.shard_map(
        body,
        mesh=mesh,
        in_specs=(
            P("narrow"),
            P(),
            P(),
            P(),
            P("narrow", "wide"),
            P(),
            P("narrow", "wide"),
            P("wide", "narrow"),
            P("narrow", "wide"),
            P("wide", "narrow"),
            P(None, "narrow", "wide"),
            P(None, "narrow", "wide"),
            P("narrow", None, "wide"),
            P("narrow", None, "wide"),
            P(),
            P(None, ("wide", "narrow")),
        ),
        out_specs=(P("narrow", "wide"), P(), P()),
        check_vma=False,
    )
```

```python
import math

import jax
import jax.numpy as jnp
from jax import lax
from jax.experimental import pallas as pl
from jax.experimental.pallas import tpu as pltpu
from jax.sharding import PartitionSpec as P

HD = 128
ROT = 32
NEG = -1e30
MESH = pl.DeviceIdType.MESH
NN = 8
NWC = 8
F32 = jnp.float32
BF16 = jnp.bfloat16
VMEM_LIMIT = 67000000


def layer_norm(rows, gain):
    values = rows.astype(F32)
    center = values - jnp.mean(values, axis=-1, keepdims=True)
    spread = jnp.mean(center * center, axis=-1, keepdims=True)
    return center * lax.rsqrt(spread + 1e-05) * gain


def pick(table, index):
    match = index[:, None] == jnp.arange(table.shape[0], dtype=jnp.int32)[None, :]
    return jnp.sum(jnp.where(match, table[None, :], 0), axis=1)


def greet(devices):
    barrier = pltpu.get_barrier_semaphore()
    for device in devices:
        pl.semaphore_signal(barrier, inc=1, device_id=device, device_id_type=MESH)
    pl.semaphore_wait(barrier, len(devices))


def others(axis, count):
    me = lax.axis_index(axis)
    return [{axis: lax.rem(me + d, count)} for d in range(1, count)]


def ids_kernel(ids_ref, out_ref, ssem, rsem, lsem):
    n = lax.axis_index("narrow")
    peers = others("narrow", NN)
    greet(peers)
    local = pltpu.make_async_copy(ids_ref, out_ref.at[n], lsem)
    local.start()
    copies = []
    for d, peer in enumerate(peers):
        copies.append(
            pltpu.make_async_remote_copy(
                src_ref=ids_ref,
                dst_ref=out_ref.at[n],
                send_sem=ssem.at[d],
                recv_sem=rsem.at[d],
                device_id=peer,
                device_id_type=MESH,
            )
        )
        copies[-1].start()
    for d, copy in enumerate(copies):
        copy.wait_send()
        copy.wait_recv()
    local.wait()


def gather_ids(token_ids):
    tile = token_ids.reshape(4, 128)
    out = pl.pallas_call(
        ids_kernel,
        out_shape=jax.ShapeDtypeStruct((NN, 4, 128), jnp.int32),
        in_specs=[pl.BlockSpec(memory_space=pltpu.VMEM)],
        out_specs=pl.BlockSpec(memory_space=pltpu.VMEM),
        scratch_shapes=[
            pltpu.SemaphoreType.DMA((NN - 1,)),
            pltpu.SemaphoreType.DMA((NN - 1,)),
            pltpu.SemaphoreType.DMA,
        ],
        compiler_params=pltpu.CompilerParams(collective_id=0, has_side_effects=True),
    )(tile)
    return out.reshape(-1)


def max_kernel(val_ref, out_ref, near, far, part, ssem, rsem):
    n = lax.axis_index("narrow")
    w = lax.axis_index("wide")
    first = others("narrow", NN)
    second = others("wide", 2 * NWC)
    greet(first + second)

    def spread(src, slots, me, peers, base):
        copies = []
        for d, peer in enumerate(peers):
            copies.append(
                pltpu.make_async_remote_copy(
                    src_ref=src,
                    dst_ref=slots.at[d],
                    send_sem=ssem.at[base + d],
                    recv_sem=rsem.at[base + d],
                    device_id=peer,
                    device_id_type=MESH,
                )
            )
            copies[-1].start()
        for copy in copies:
            copy.wait_recv()
        return copies

    sent = spread(val_ref, near, n, first, 0)
    best = val_ref[...]
    for d in range(NN - 1):
        best = jnp.maximum(best, near[d])
    part[...] = best
    sent += spread(part, far, w, second, NN - 1)
    for d in range(2 * NWC - 1):
        best = jnp.maximum(best, far[d])
    out_ref[...] = best
    for copy in sent:
        copy.wait_send()


def max_over_all(values):
    tile = jnp.broadcast_to(values[:, None], (8, 128))
    out = pl.pallas_call(
        max_kernel,
        out_shape=jax.ShapeDtypeStruct((8, 128), F32),
        in_specs=[pl.BlockSpec(memory_space=pltpu.VMEM)],
        out_specs=pl.BlockSpec(memory_space=pltpu.VMEM),
        scratch_shapes=[
            pltpu.VMEM((NN - 1, 8, 128), F32),
            pltpu.VMEM((2 * NWC - 1, 8, 128), F32),
            pltpu.VMEM((8, 128), F32),
            pltpu.SemaphoreType.DMA((22,)),
            pltpu.SemaphoreType.DMA((22,)),
        ],
        compiler_params=pltpu.CompilerParams(collective_id=2, has_side_effects=True),
    )(tile)
    return out[:, 0]


class Spread:
    def __init__(self, own, buf, base, sems, place):
        self.own, self.buf, self.base = own, buf, base
        self.ssem, self.rsem, self.lsem = sems
        self.n, self.w, self.x, self.c, self.home, self.away, self.swap, self.sibling = place
        self.first = 2 * self.x + self.c
        self.arrivals = [lax.rem(self.first + NN - d, NN) for d in (2, 6, 4)]

    def copy(self, i, src, m, dst):
        return pltpu.make_async_remote_copy(
            src_ref=src,
            dst_ref=self.buf.at[m],
            send_sem=self.ssem.at[self.base + i],
            recv_sem=self.rsem.at[self.base + i],
            device_id=dst,
            device_id_type=MESH,
        )

    def fan(self, src):
        for i, d in enumerate((2, 6)):
            self.copy(i, src, self.first, {"narrow": lax.rem(self.n + d, NN)}).start()
        self.copy(3, src, self.first, self.sibling).start()

    def local(self):
        return pltpu.make_async_copy(self.own, self.buf.at[self.n], self.lsem)

    def z(self):
        return self.copy(7, self.own, self.n, self.swap)

    def start_home(self):
        @pl.when(self.home)
        def _():
            self.local().start()
            self.fan(self.own)

    def start_away(self):
        @pl.when(self.away)
        def _():
            self.z().start()

    def relay(self):
        @pl.when(self.away)
        def _():
            self.copy(7, self.own, self.first, self.swap).wait_recv()
            self.fan(self.buf.at[self.first])

        @pl.when(self.home)
        def _():
            self.local().wait()

    def half(self, h, m):
        size = self.buf.shape[1] // 2
        part = self.buf.at[m, pl.ds(h * size, size)]
        return pltpu.make_async_remote_copy(
            src_ref=part,
            dst_ref=part,
            send_sem=self.ssem.at[self.base + (2, 8)[h]],
            recv_sem=self.rsem.at[self.base + (2, 8)[h]],
            device_id={"narrow": lax.rem(self.n + (2, 6)[h], NN)},
            device_id_type=MESH,
        )

    def pass_on(self):
        for i, m in enumerate(self.arrivals[:2]):
            self.copy(i, self.buf.at[m], m, self.sibling).wait_recv()
            self.half(i, m).start()
            self.copy(4 + i, self.buf.at[m], m, self.sibling).start()

    def share(self):
        m = self.arrivals[2]
        for h in range(2):
            self.half(h, m).wait_recv()
        self.copy(6, self.buf.at[m], m, self.sibling).start()

    def others(self):
        flip = 1 - 2 * self.c
        return [self.first + flip] + [m + flip for m in self.arrivals]

    def complete(self):
        for i, m in enumerate(self.others()):
            self.copy(3 + i, self.buf.at[m], m, self.sibling).wait_recv()

    def finish(self):
        for i in (0, 1, 3, 4, 5, 6):
            self.copy(i, self.buf.at[self.first], self.first, self.sibling).wait_send()
        for h in range(2):
            self.half(h, self.first).wait_send()

        @pl.when(self.away)
        def _():
            self.z().wait_send()


def layer_kernel(
    rows,
    wq_in,
    wu_in,
    wd_in,
    wo_in,
    pk_in,
    pv_in,
    sk_in,
    sv_in,
    owner,
    gains,
    cos_t,
    sin_a,
    sin_b,
    bias,
    out_ref,
    last_ref,
    wq,
    wu,
    wd,
    wo,
    pk,
    pv,
    sk,
    sv,
    emb,
    resid,
    xs,
    na,
    nm,
    qkv,
    scores,
    probs,
    attn,
    acc,
    hid,
    ry_s,
    ry_r,
    rz_s,
    rz_r,
    last_n,
    last_w,
    ssem,
    rsem,
    lsem,
):
    n = lax.axis_index("narrow")
    w = lax.axis_index("wide")
    c = lax.rem(w, 2)
    wc = lax.div(w, 2)
    y, zl = lax.div(wc, 2), lax.rem(wc, 2)
    x, zh = lax.div(n, 2), lax.rem(n, 2)
    home, away = zh == c, zh != c
    n_flip, w_flip = n + 1 - 2 * zh, w + 1 - 2 * c
    sibling = {"wide": w_flip}
    swap = {"narrow": n_flip, "wide": w_flip}
    tokens, feats = out_ref.shape
    scale = 1.0 / math.sqrt(HD)
    wide = 2 * NWC

    def remote(src, dst, i, device, j=None):
        return pltpu.make_async_remote_copy(
            src_ref=src,
            dst_ref=dst,
            send_sem=ssem.at[i],
            recv_sem=rsem.at[i if j is None else j],
            device_id=device,
            device_id_type=MESH,
        )

    greeted = []
    for d in range(NN):
        for e in range(2):
            if d or e:
                greeted.append({"narrow": lax.rem(n + d, NN), "wide": 2 * wc + lax.rem(c + e, 2)})
    for d in range(2):
        for e in range(1, NWC):
            for f in range(2):
                greeted.append({"narrow": 2 * x + lax.rem(zh + d, 2), "wide": 2 * lax.rem(wc + e, NWC) + f})
    greet(greeted)

    place = (n, w, x, c, home, away, swap, sibling)
    names = ["q", "d", "o", "u"]
    spreads = {}
    for k, (name, own, buf) in enumerate(zip(names, (wq_in, wd_in, wo_in, wu_in), (wq, wd, wo, wu))):
        spreads[name] = Spread(own, buf, 9 * k, (ssem, rsem, lsem.at[k]), place)
    sq, sd, so, su = (spreads[name] for name in names)
    at = 36
    sends = []

    emb_at = at
    at += 7
    own_rows = pltpu.make_async_copy(rows.at[pl.ds(pl.multiple_of(n * tokens, tokens), tokens)], emb.at[n], lsem.at[4])
    own_rows.start()
    for d in range(1, NN):
        m = lax.rem(n + d, NN)
        copy = remote(rows.at[pl.ds(pl.multiple_of(m * tokens, tokens), tokens)], emb.at[n], emb_at + d - 1, {"narrow": m})
        copy.start()
        sends.append(copy)
    sq.start_home()
    sq.start_away()
    sd.start_home()

    own_rows.wait()
    for d in range(1, NN):
        src = lax.rem(n + NN - d, NN)
        remote(emb.at[src], emb.at[src], emb_at + d - 1, sibling).wait_recv()

    @pl.loop(0, tokens // 64)
    def _(i):
        r = pl.ds(pl.multiple_of(i * 64, 64), 64)
        who = owner[r, :]
        total = emb[0, r, :]
        for m in range(1, NN):
            total = jnp.where(who == m, emb[m, r, :], total)
        resid[r, :] = total

        @pl.when(home)
        def _():
            xs[w, r, :] = total

    z_at = at
    at += 4
    y_at = at
    at += 12

    def over_z(d, e):
        m = {"narrow": 2 * x + lax.rem(zh + d, 2), "wide": (2 * y + lax.rem(zl + e, 2)) * 2 + zh}
        return remote(resid, xs.at[w], z_at + 2 * d + e, m, z_at + 2 * zl + c)

    for d, e in ((0, 1), (1, 0), (1, 1)):
        over_z(d, e).start()

    @pl.when(away)
    def _():
        over_z(0, 0).start()

    sq.relay()
    sd.start_away()

    suffix_at = at
    at += 2
    suffix = ((sk_in.at[0], sk), (sv_in.at[0], sv))

    @pl.when(home)
    def _():
        for j, (src, dst) in enumerate(suffix):
            pltpu.make_async_copy(src, dst, lsem.at[5 + j]).start()

    @pl.when(away)
    def _():
        for j, (src, dst) in enumerate(suffix):
            remote(src, dst, suffix_at + j, swap).start()

    def over_y(i, d):
        block = 4 * y + i
        m = {"wide": (2 * lax.rem(y + d, 4) + zl) * 2 + c}
        return remote(xs.at[block], xs.at[block], y_at + 4 * (d - 1) + i, m)

    for i in range(4):
        block = 4 * y + i

        @pl.when(jnp.logical_not(jnp.logical_and(home, 2 * zl + c == i)))
        def _():
            remote(xs.at[block], xs.at[block], z_at + i, sibling).wait_recv()

        for d in range(1, 4):
            over_y(i, d).start()

    pre_at = at
    at += 16
    prefix = ((pk_in, pk), (pv_in, pv))

    def over_x(j, d, e):
        src, dst = prefix[j]
        px, pc = lax.rem(x + d, 4), lax.rem(c + e, 2)
        m = {"narrow": 2 * px + c, "wide": 2 * wc + pc}
        return remote(src.at[2 * px + pc], dst.at[n], pre_at + 8 * j + 2 * d + e, m, pre_at + 8 * j + 4 * zh + d)

    for j in range(2):
        for d in range(4):
            for e in range(2):
                if d or e:
                    over_x(j, d, e).start()

    @pl.when(home)
    def _():
        for j, (src, dst) in enumerate(prefix):
            pltpu.make_async_copy(src.at[n], dst.at[n], lsem.at[7 + j]).start()

    @pl.when(away)
    def _():
        for j in range(2):
            over_x(j, 0, 0).start()

    so.start_home()
    so.start_away()
    su.start_home()
    su.start_away()
    sq.pass_on()
    sd.relay()
    for i in range(4):
        for d in range(1, 4):
            block = 4 * lax.rem(y + 4 - d, 4) + i
            remote(xs.at[block], xs.at[block], y_at + 4 * (d - 1) + i, sibling).wait_recv()

    sq.share()
    total_feats = wide * feats

    @pl.loop(0, tokens // 32)
    def _(i):
        r = pl.ds(pl.multiple_of(i * 32, 32), 32)
        total = xs[0, r, :].astype(F32)
        for m in range(1, wide):
            total = total + xs[m, r, :].astype(F32)
        mean = jnp.sum(total, axis=-1, keepdims=True) * (1.0 / total_feats)
        var = jnp.zeros_like(total)
        for m in range(wide):
            center = xs[m, r, :].astype(F32) - mean
            var = var + center * center
        inv = lax.rsqrt(jnp.sum(var, axis=-1, keepdims=True) * (1.0 / total_feats) + 1e-05)
        for m in range(wide):
            cols = slice(m * feats, (m + 1) * feats)
            normed = (xs[m, r, :].astype(F32) - mean) * inv
            na[r, cols] = (normed * gains[0:1, cols]).astype(BF16)
            nm[r, cols] = (normed * gains[1:2, cols]).astype(BF16)

    so.relay()
    su.relay()
    sd.pass_on()
    sq.complete()

    @pl.loop(0, wq.shape[2] // 256)
    def _(j):
        cols = pl.ds(pl.multiple_of(j * 256, 256), 256)
        weight = wq[:, :, cols].reshape(na.shape[1], 256)
        qkv[:, cols] = jnp.dot(na[...], weight, preferred_element_type=F32).astype(BF16)

    sd.share()

    @pl.loop(0, 4)
    def _(i):
        r = pl.ds(pl.multiple_of(i * 128, 128), 128)
        for h in range(2):
            for t in range(2):
                cols = slice((3 * h + t) * HD, (3 * h + t + 1) * HD)
                v = qkv[r, cols].astype(F32)
                turned = v * cos_t[r, :] + pltpu.roll(v, HD - ROT // 2, 1) * sin_a[r, :] + pltpu.roll(v, ROT // 2, 1) * sin_b[r, :]
                qkv[r, cols] = turned.astype(BF16)

    @pl.when(home)
    def _():
        for j, (src, dst) in enumerate(suffix):
            pltpu.make_async_copy(src, dst, lsem.at[5 + j]).wait()

    @pl.when(away)
    def _():
        for j, (src, dst) in enumerate(suffix):
            remote(src, dst, suffix_at + j, swap).wait_recv()

    for j, (src, dst) in enumerate(prefix):
        for sz in range(2):
            for d in range(4):
                m = 2 * lax.rem(x + 4 - d, 4) + sz
                arrival = remote(dst.at[m], dst.at[m], pre_at, sibling, pre_at + 8 * j + 4 * sz + d)
                if d:
                    arrival.wait_recv()
                else:
                    mine = jnp.logical_and(home, zh == sz)

                    @pl.when(mine)
                    def _():
                        pltpu.make_async_copy(src.at[n], dst.at[n], lsem.at[7 + j]).wait()

                    @pl.when(jnp.logical_not(mine))
                    def _():
                        arrival.wait_recv()

    pre_len = pk.shape[0] * pk.shape[1]
    suf_len = sk.shape[0]
    qc = scores.shape[0]

    def attend(h):
        hc = slice(h * HD, (h + 1) * HD)
        q_cols = slice(3 * h * HD, (3 * h + 1) * HD)
        k_cols = slice((3 * h + 1) * HD, (3 * h + 2) * HD)
        v_cols = slice((3 * h + 2) * HD, (3 * h + 3) * HD)

        @pl.loop(0, tokens // qc)
        def _(i):
            r = pl.ds(pl.multiple_of(i * qc, qc), qc)
            q = qkv[r, q_cols]

            def score(keys):
                return lax.dot_general(q, keys, (((1,), (1,)), ((), ())), preferred_element_type=F32) * scale

            keys = pk[:, :, hc].reshape(pre_len, HD)
            s = score(keys) + bias[0:1, 0:pre_len]
            scores[:, 0:pre_len] = s
            top = jnp.max(s, axis=-1, keepdims=True)
            for b in range(suf_len // 512):
                lo = pre_len + b * 512
                s = score(sk[b * 512 : (b + 1) * 512, hc]) + bias[0:1, lo : lo + 512]
                scores[:, lo : lo + 512] = s
                top = jnp.maximum(top, jnp.max(s, axis=-1, keepdims=True))
            lo = pre_len + suf_len
            s = score(qkv[:, k_cols])
            row = lax.broadcasted_iota(jnp.int32, s.shape, 0) + i * qc
            col = lax.broadcasted_iota(jnp.int32, s.shape, 1)
            s = jnp.where(row >= col, s, NEG)
            scores[:, lo : lo + tokens] = s
            top = jnp.maximum(top, jnp.max(s, axis=-1, keepdims=True))
            den = jnp.zeros((qc, 1), F32)
            for b in range(scores.shape[1] // 512):
                p = jnp.exp(scores[:, b * 512 : (b + 1) * 512] - top)
                den = den + jnp.sum(p, axis=-1, keepdims=True)
                probs[:, b * 512 : (b + 1) * 512] = p.astype(BF16)
            num = jnp.dot(probs[:, 0:pre_len], pv[:, :, hc].reshape(pre_len, HD), preferred_element_type=F32)
            num = num + jnp.dot(probs[:, pre_len:lo], sv[:, hc], preferred_element_type=F32)
            num = num + jnp.dot(probs[:, lo : lo + tokens], qkv[:, v_cols], preferred_element_type=F32)
            attn[r, hc] = (num / den).astype(BF16)

    attend(0)
    so.pass_on()
    su.pass_on()
    attend(1)
    so.share()
    su.share()

    def up_rows(m, fresh):
        k = pl.ds(pl.multiple_of(m * wu.shape[1], wu.shape[1]), wu.shape[1])

        @pl.loop(0, wu.shape[2] // 256)
        def _(j):
            cols = pl.ds(pl.multiple_of(j * 256, 256), 256)
            part = jnp.dot(nm[:, k], wu[m, :, cols], preferred_element_type=F32)
            if fresh:
                acc[:, cols] = part
            else:
                acc[:, cols] += part

    up_rows(su.first, True)
    for m in su.arrivals:
        up_rows(m, False)
    su.complete()
    for m in su.others():
        up_rows(m, False)

    @pl.loop(0, tokens // 64)
    def _(i):
        r = pl.ds(pl.multiple_of(i * 64, 64), 64)
        u = acc[r, :]
        hid[r, :] = (0.5 * u * (1.0 + lax.erf(u * math.sqrt(0.5)))).astype(BF16)

    sd.complete()
    so.complete()

    sum_at = at
    at += 3
    part_at = at
    at += 4
    span = wd.shape[2]

    def terms(m):
        return jnp.dot(hid[...], wd[m], preferred_element_type=F32) + jnp.dot(
            attn[...], wo[m], preferred_element_type=F32
        )

    def to_y(r):
        m = {"wide": (2 * lax.rem(y + 1 + r, 4) + zl) * 2 + c}
        return remote(ry_s.at[r], ry_r.at[r], sum_at + r, m)

    for r in range(3):

        @pl.loop(0, 2)
        def _(j):
            cols = pl.ds(pl.multiple_of(j * span, span), span)
            ry_s[r, :, cols] = terms(2 * lax.rem(y + 1 + r, 4) + j).astype(BF16)

        to_y(r).start()

    @pl.loop(0, 2)
    def _(j):
        cols = pl.ds(pl.multiple_of(j * span, span), span)
        acc[:, cols] = terms(2 * y + j)

    for r in range(3):
        to_y(r).wait_recv()
    spot = 2 * zh + zl

    def to_z(i):
        m = {"narrow": 2 * x + c, "wide": 4 * y + i}
        return remote(rz_s.at[i], rz_r.at[spot], part_at + i, m, part_at + spot)

    for i in range(4):
        cols = slice(i * feats, (i + 1) * feats)

        @pl.loop(0, tokens // 64)
        def _(k):
            r = pl.ds(pl.multiple_of(k * 64, 64), 64)
            total = acc[r, cols]
            for m in range(3):
                total = total + ry_r[m, r, cols].astype(F32)
            rz_s[i, r, :] = total.astype(BF16)

        mine = jnp.logical_and(home, 2 * zl + c == i)

        @pl.when(jnp.logical_not(mine))
        def _():
            to_z(i).start()

        @pl.when(mine)
        def _():
            rz_r[spot] = rz_s[i]

    for i in range(4):

        @pl.when(jnp.logical_not(jnp.logical_and(home, spot == i)))
        def _():
            remote(rz_r.at[i], rz_r.at[i], part_at, sibling, part_at + i).wait_recv()

    @pl.loop(0, tokens // 64)
    def _(i):
        r = pl.ds(pl.multiple_of(i * 64, 64), 64)
        total = rz_r[0, r, :].astype(F32)
        for m in range(1, 4):
            total = total + rz_r[m, r, :].astype(F32)
        out_ref[r, :] = (resid[r, :].astype(F32) + total).astype(BF16)

    tail = out_ref[tokens - 16 : tokens, :].astype(F32)
    last_n[n] = jnp.broadcast_to(tail[15:16, :], (8, feats))
    ln_at = at
    at += 7
    for d in range(1, NN):
        copy = remote(last_n.at[n], last_n.at[n], ln_at + d - 1, {"narrow": lax.rem(n + d, NN)})
        copy.start()
        sends.append(copy)
    for d in range(1, NN):
        src = lax.rem(n + NN - d, NN)
        remote(last_n.at[src], last_n.at[src], ln_at + d - 1, sibling).wait_recv()
    pick_row = lax.broadcasted_iota(jnp.int32, (8, feats), 0)
    eight = last_n[0]
    for m in range(1, NN):
        eight = jnp.where(pick_row == m, last_n[m], eight)
    last_w[w] = eight
    lw_at = at
    at += 15
    for d in range(1, wide):
        copy = remote(last_w.at[w], last_w.at[w], lw_at + d - 1, {"wide": lax.rem(w + d, wide)})
        copy.start()
        sends.append(copy)
    for d in range(1, wide):
        src = lax.rem(w + wide - d, wide)
        remote(last_w.at[src], last_w.at[src], lw_at + d - 1, sibling).wait_recv()
    for m in range(wide):
        last_ref[:, m * feats : (m + 1) * feats] = last_w[m]

    for copy in sends:
        copy.wait_send()
    for name in names:
        spreads[name].finish()
    for d, e in ((0, 1), (1, 0), (1, 1)):
        over_z(d, e).wait_send()
    for i in range(4):
        for d in range(1, 4):
            over_y(i, d).wait_send()
    for j in range(2):
        for d in range(4):
            for e in range(2):
                if d or e:
                    over_x(j, d, e).wait_send()

    @pl.when(away)
    def _():
        over_z(0, 0).wait_send()
        for j, (src, dst) in enumerate(suffix):
            remote(src, dst, suffix_at + j, swap).wait_send()
        for j in range(2):
            over_x(j, 0, 0).wait_send()

    for r in range(3):
        to_y(r).wait_send()
    for i in range(4):

        @pl.when(jnp.logical_not(jnp.logical_and(home, 2 * zl + c == i)))
        def _():
            to_z(i).wait_send()


def layer(rows, wq, wu, wd, wo, pk, pv, sk, sv, owner, gains, cos_t, sin_a, sin_b, bias):
    tokens = rows.shape[0] // NN
    feats = rows.shape[1]
    dim = 2 * NWC * feats
    keys = bias.shape[1]
    qc = 256
    vm = pltpu.VMEM
    anywhere = pl.BlockSpec(memory_space=pl.ANY)
    inside = pl.BlockSpec(memory_space=pltpu.VMEM)
    four = (4, tokens, feats)
    groups = (3, tokens, 4 * feats)
    return pl.pallas_call(
        layer_kernel,
        out_shape=(
            jax.ShapeDtypeStruct((tokens, feats), BF16),
            jax.ShapeDtypeStruct((NN, dim), F32),
        ),
        in_specs=[anywhere] * 9 + [inside] * 6,
        out_specs=(inside, inside),
        scratch_shapes=[
            vm((NN,) + wq.shape, BF16),
            vm((NN,) + wu.shape, BF16),
            vm((NN,) + wd.shape, BF16),
            vm((NN,) + wo.shape, BF16),
            vm(pk.shape, BF16),
            vm(pv.shape, BF16),
            vm(sk.shape[1:], BF16),
            vm(sv.shape[1:], BF16),
            vm((NN, tokens, feats), BF16),
            vm((tokens, feats), BF16),
            vm((2 * NWC, tokens, feats), BF16),
            vm((tokens, dim), BF16),
            vm((tokens, dim), BF16),
            vm((tokens, wq.shape[1]), BF16),
            vm((qc, keys), F32),
            vm((qc, keys), BF16),
            vm((tokens, feats), BF16),
            vm((tokens, wu.shape[1]), F32),
            vm((tokens, wu.shape[1]), BF16),
            vm(groups, BF16),
            vm(groups, BF16),
            vm(four, BF16),
            vm(four, BF16),
            vm((NN, 8, feats), F32),
            vm((2 * NWC, 8, feats), F32),
            pltpu.SemaphoreType.DMA((112,)),
            pltpu.SemaphoreType.DMA((112,)),
            pltpu.SemaphoreType.DMA((9,)),
        ],
        compiler_params=pltpu.CompilerParams(
            collective_id=1, has_side_effects=True, vmem_limit_bytes=VMEM_LIMIT
        ),
    )(rows, wq, wu, wd, wo, pk, pv, sk, sv, owner, gains, cos_t, sin_a, sin_b, bias)


def body(
    token_ids,
    group_ids,
    prefix_lengths,
    cached_lengths,
    embedding,
    ln_gains,
    qkv_weight,
    out_weight,
    up_weight,
    down_weight,
    prefix_keys,
    prefix_values,
    suffix_keys,
    suffix_values,
    final_gain,
    head_weight,
):
    n = lax.axis_index("narrow")
    stretch = token_ids.shape[0]
    all_ids = gather_ids(token_ids)
    vocab_rows = embedding.shape[0]
    local_ids = all_ids - n * vocab_rows
    rows = embedding.at[jnp.clip(local_ids, 0, vocab_rows - 1)].get(mode="promise_in_bounds")
    owner = jnp.broadcast_to((token_ids // vocab_rows)[:, None], (stretch, embedding.shape[1]))

    second = (group_ids == 1)[:, None, None]
    pk = jnp.where(second, prefix_keys[1][None], prefix_keys[0][None])
    pv = jnp.where(second, prefix_values[1][None], prefix_values[0][None])
    me = (2 * (n // 2) + lax.axis_index("wide") % 2)[None]
    group = pick(group_ids, me)
    far = pick(prefix_lengths, group)[0]
    cached = pick(cached_lengths, me)[0]
    places = (far + cached + jnp.arange(stretch, dtype=jnp.int32)).astype(F32)
    half = ROT // 2
    freqs = jnp.power(10000.0, -(jnp.arange(half).astype(F32) * 2.0 / ROT))
    angles = places[:, None] * freqs[None, :]
    cosine, sine = jnp.cos(angles), jnp.sin(angles)
    rest = HD - ROT
    cos_t = jnp.concatenate([cosine, cosine, jnp.ones((stretch, rest), F32)], axis=1)
    sin_a = jnp.concatenate([-sine, jnp.zeros((stretch, HD - half), F32)], axis=1)
    sin_b = jnp.concatenate([jnp.zeros((stretch, half), F32), sine, jnp.zeros((stretch, rest), F32)], axis=1)
    pre = NN * prefix_keys.shape[1]
    ok = jnp.concatenate(
        [
            jnp.arange(pre, dtype=jnp.int32) < far,
            jnp.arange(suffix_keys.shape[1], dtype=jnp.int32) < cached,
            jnp.ones((stretch,), bool),
        ]
    )
    bias = jnp.broadcast_to(jnp.where(ok, 0.0, NEG).astype(F32)[None, :], (8, ok.shape[0]))

    hidden_out, last_values = layer(
        rows,
        qkv_weight,
        up_weight,
        down_weight,
        out_weight,
        pk,
        pv,
        suffix_keys,
        suffix_values,
        owner,
        ln_gains,
        cos_t,
        sin_a,
        sin_b,
        bias,
    )
    last_rms = jnp.sqrt(jnp.mean(last_values * last_values, axis=-1))
    final_rows = layer_norm(last_values, final_gain).astype(BF16)
    logits = jnp.dot(final_rows, head_weight, preferred_element_type=F32)
    max_logit = max_over_all(jnp.max(logits, axis=-1))
    return (hidden_out, last_rms, max_logit)


def solution(mesh):
    return jax.shard_map(
        body,
        mesh=mesh,
        in_specs=(
            P("narrow"),
            P(),
            P(),
            P(),
            P("narrow", "wide"),
            P(),
            P("narrow", "wide"),
            P("wide", "narrow"),
            P("narrow", "wide"),
            P("wide", "narrow"),
            P(None, "narrow", "wide"),
            P(None, "narrow", "wide"),
            P("narrow", None, "wide"),
            P("narrow", None, "wide"),
            P(),
            P(None, ("wide", "narrow")),
        ),
        out_specs=(P("narrow", "wide"), P(), P()),
        check_vma=False,
    )
```

```python
import math

import jax
import jax.numpy as jnp
from jax import lax
from jax.experimental import pallas as pl
from jax.experimental.pallas import tpu as pltpu
from jax.sharding import PartitionSpec as P

HD = 128
ROT = 32
NEG = -1e30
MESH = pl.DeviceIdType.MESH
NN = 8
NWC = 8
F32 = jnp.float32
BF16 = jnp.bfloat16
VMEM_LIMIT = 67000000


def layer_norm(rows, gain):
    values = rows.astype(F32)
    center = values - jnp.mean(values, axis=-1, keepdims=True)
    spread = jnp.mean(center * center, axis=-1, keepdims=True)
    return center * lax.rsqrt(spread + 1e-05) * gain


def pick(table, index):
    match = index[:, None] == jnp.arange(table.shape[0], dtype=jnp.int32)[None, :]
    return jnp.sum(jnp.where(match, table[None, :], 0), axis=1)


def greet(devices):
    barrier = pltpu.get_barrier_semaphore()
    for device in devices:
        pl.semaphore_signal(barrier, inc=1, device_id=device, device_id_type=MESH)
    pl.semaphore_wait(barrier, len(devices))


def others(axis, count):
    me = lax.axis_index(axis)
    return [{axis: lax.rem(me + d, count)} for d in range(1, count)]


def ids_kernel(ids_ref, out_ref, ssem, rsem, lsem):
    n = lax.axis_index("narrow")
    peers = others("narrow", NN)
    greet(peers)
    local = pltpu.make_async_copy(ids_ref, out_ref.at[n], lsem)
    local.start()
    copies = []
    for d, peer in enumerate(peers):
        copies.append(
            pltpu.make_async_remote_copy(
                src_ref=ids_ref,
                dst_ref=out_ref.at[n],
                send_sem=ssem.at[d],
                recv_sem=rsem.at[d],
                device_id=peer,
                device_id_type=MESH,
            )
        )
        copies[-1].start()
    for d, copy in enumerate(copies):
        copy.wait_send()
        copy.wait_recv()
    local.wait()


def gather_ids(token_ids):
    tile = token_ids.reshape(4, 128)
    out = pl.pallas_call(
        ids_kernel,
        out_shape=jax.ShapeDtypeStruct((NN, 4, 128), jnp.int32),
        in_specs=[pl.BlockSpec(memory_space=pltpu.VMEM)],
        out_specs=pl.BlockSpec(memory_space=pltpu.VMEM),
        scratch_shapes=[
            pltpu.SemaphoreType.DMA((NN - 1,)),
            pltpu.SemaphoreType.DMA((NN - 1,)),
            pltpu.SemaphoreType.DMA,
        ],
        compiler_params=pltpu.CompilerParams(collective_id=0, has_side_effects=True),
    )(tile)
    return out.reshape(-1)


def max_kernel(val_ref, out_ref, near, far, part, ssem, rsem):
    n = lax.axis_index("narrow")
    w = lax.axis_index("wide")
    first = others("narrow", NN)
    second = others("wide", 2 * NWC)
    greet(first + second)

    def spread(src, slots, me, peers, base):
        copies = []
        for d, peer in enumerate(peers):
            copies.append(
                pltpu.make_async_remote_copy(
                    src_ref=src,
                    dst_ref=slots.at[d],
                    send_sem=ssem.at[base + d],
                    recv_sem=rsem.at[base + d],
                    device_id=peer,
                    device_id_type=MESH,
                )
            )
            copies[-1].start()
        for copy in copies:
            copy.wait_recv()
        return copies

    sent = spread(val_ref, near, n, first, 0)
    best = val_ref[...]
    for d in range(NN - 1):
        best = jnp.maximum(best, near[d])
    part[...] = best
    sent += spread(part, far, w, second, NN - 1)
    for d in range(2 * NWC - 1):
        best = jnp.maximum(best, far[d])
    out_ref[...] = best
    for copy in sent:
        copy.wait_send()


def max_over_all(values):
    tile = jnp.broadcast_to(values[:, None], (8, 128))
    out = pl.pallas_call(
        max_kernel,
        out_shape=jax.ShapeDtypeStruct((8, 128), F32),
        in_specs=[pl.BlockSpec(memory_space=pltpu.VMEM)],
        out_specs=pl.BlockSpec(memory_space=pltpu.VMEM),
        scratch_shapes=[
            pltpu.VMEM((NN - 1, 8, 128), F32),
            pltpu.VMEM((2 * NWC - 1, 8, 128), F32),
            pltpu.VMEM((8, 128), F32),
            pltpu.SemaphoreType.DMA((22,)),
            pltpu.SemaphoreType.DMA((22,)),
        ],
        compiler_params=pltpu.CompilerParams(collective_id=2, has_side_effects=True),
    )(tile)
    return out[:, 0]


class Spread:
    def __init__(self, own, buf, base, sems, place):
        self.own, self.buf, self.base = own, buf, base
        self.ssem, self.rsem, self.lsem = sems
        self.n, self.w, self.x, self.c, self.home, self.away, self.swap, self.sibling = place
        self.first = 2 * self.x + self.c
        self.arrivals = [lax.rem(self.first + NN - d, NN) for d in (2, 6, 4)]

    def copy(self, i, src, m, dst):
        return pltpu.make_async_remote_copy(
            src_ref=src,
            dst_ref=self.buf.at[m],
            send_sem=self.ssem.at[self.base + i],
            recv_sem=self.rsem.at[self.base + i],
            device_id=dst,
            device_id_type=MESH,
        )

    def fan(self, src):
        for i, d in enumerate((2, 6)):
            self.copy(i, src, self.first, {"narrow": lax.rem(self.n + d, NN)}).start()
        self.copy(3, src, self.first, self.sibling).start()

    def local(self):
        return pltpu.make_async_copy(self.own, self.buf.at[self.n], self.lsem)

    def z(self):
        return self.copy(7, self.own, self.n, self.swap)

    def start_home(self):
        @pl.when(self.home)
        def _():
            self.local().start()
            self.fan(self.own)

    def start_away(self):
        @pl.when(self.away)
        def _():
            self.z().start()

    def relay(self):
        @pl.when(self.away)
        def _():
            self.copy(7, self.own, self.first, self.swap).wait_recv()
            self.fan(self.buf.at[self.first])

        @pl.when(self.home)
        def _():
            self.local().wait()

    def half(self, h, m):
        size = self.buf.shape[1] // 2
        part = self.buf.at[m, pl.ds(h * size, size)]
        return pltpu.make_async_remote_copy(
            src_ref=part,
            dst_ref=part,
            send_sem=self.ssem.at[self.base + (2, 8)[h]],
            recv_sem=self.rsem.at[self.base + (2, 8)[h]],
            device_id={"narrow": lax.rem(self.n + (2, 6)[h], NN)},
            device_id_type=MESH,
        )

    def pass_on(self):
        for i, m in enumerate(self.arrivals[:2]):
            self.copy(i, self.buf.at[m], m, self.sibling).wait_recv()
            self.half(i, m).start()
            self.copy(4 + i, self.buf.at[m], m, self.sibling).start()

    def share(self):
        m = self.arrivals[2]
        for h in range(2):
            self.half(h, m).wait_recv()
        self.copy(6, self.buf.at[m], m, self.sibling).start()

    def others(self):
        flip = 1 - 2 * self.c
        return [self.first + flip] + [m + flip for m in self.arrivals]

    def complete(self):
        for i, m in enumerate(self.others()):
            self.copy(3 + i, self.buf.at[m], m, self.sibling).wait_recv()

    def finish(self):
        for i in (0, 1, 3, 4, 5, 6):
            self.copy(i, self.buf.at[self.first], self.first, self.sibling).wait_send()
        for h in range(2):
            self.half(h, self.first).wait_send()

        @pl.when(self.away)
        def _():
            self.z().wait_send()


def layer_kernel(
    rows,
    wq_in,
    wu_in,
    wd_in,
    wo_in,
    pk_in,
    pv_in,
    sk_in,
    sv_in,
    owner,
    gains,
    cos_t,
    sin_a,
    sin_b,
    bias,
    out_ref,
    last_ref,
    wq,
    wu,
    wd,
    wo,
    pk,
    pv,
    sk,
    sv,
    emb,
    resid,
    xs,
    na,
    nm,
    qkv,
    scores,
    probs,
    attn,
    acc,
    hid,
    ry_s,
    ry_r,
    rz_s,
    rz_r,
    last_n,
    last_w,
    ssem,
    rsem,
    lsem,
):
    n = lax.axis_index("narrow")
    w = lax.axis_index("wide")
    c = lax.rem(w, 2)
    wc = lax.div(w, 2)
    y, zl = lax.div(wc, 2), lax.rem(wc, 2)
    x, zh = lax.div(n, 2), lax.rem(n, 2)
    home, away = zh == c, zh != c
    n_flip, w_flip = n + 1 - 2 * zh, w + 1 - 2 * c
    sibling = {"wide": w_flip}
    swap = {"narrow": n_flip, "wide": w_flip}
    tokens, feats = out_ref.shape
    scale = 1.0 / math.sqrt(HD)
    wide = 2 * NWC

    def remote(src, dst, i, device, j=None):
        return pltpu.make_async_remote_copy(
            src_ref=src,
            dst_ref=dst,
            send_sem=ssem.at[i],
            recv_sem=rsem.at[i if j is None else j],
            device_id=device,
            device_id_type=MESH,
        )

    greeted = []
    for d in range(NN):
        for e in range(2):
            if d or e:
                greeted.append({"narrow": lax.rem(n + d, NN), "wide": 2 * wc + lax.rem(c + e, 2)})
    for d in range(2):
        for e in range(1, NWC):
            for f in range(2):
                greeted.append({"narrow": 2 * x + lax.rem(zh + d, 2), "wide": 2 * lax.rem(wc + e, NWC) + f})
    greet(greeted)

    place = (n, w, x, c, home, away, swap, sibling)
    names = ["q", "d", "o", "u"]
    spreads = {}
    for k, (name, own, buf) in enumerate(zip(names, (wq_in, wd_in, wo_in, wu_in), (wq, wd, wo, wu))):
        spreads[name] = Spread(own, buf, 9 * k, (ssem, rsem, lsem.at[k]), place)
    sq, sd, so, su = (spreads[name] for name in names)
    at = 36
    sends = []

    emb_at = at
    at += 7
    own_rows = pltpu.make_async_copy(rows.at[pl.ds(pl.multiple_of(n * tokens, tokens), tokens)], emb.at[n], lsem.at[4])
    own_rows.start()
    for d in range(1, NN):
        m = lax.rem(n + d, NN)
        copy = remote(rows.at[pl.ds(pl.multiple_of(m * tokens, tokens), tokens)], emb.at[n], emb_at + d - 1, {"narrow": m})
        copy.start()
        sends.append(copy)
    sq.start_home()
    sq.start_away()
    sd.start_home()

    own_rows.wait()
    for d in range(1, NN):
        src = lax.rem(n + NN - d, NN)
        remote(emb.at[src], emb.at[src], emb_at + d - 1, sibling).wait_recv()

    @pl.loop(0, tokens // 64)
    def _(i):
        r = pl.ds(pl.multiple_of(i * 64, 64), 64)
        who = owner[r, :]
        total = emb[0, r, :]
        for m in range(1, NN):
            total = jnp.where(who == m, emb[m, r, :], total)
        resid[r, :] = total

        @pl.when(home)
        def _():
            xs[w, r, :] = total

    z_at = at
    at += 4
    y_at = at
    at += 12

    def over_z(d, e):
        m = {"narrow": 2 * x + lax.rem(zh + d, 2), "wide": (2 * y + lax.rem(zl + e, 2)) * 2 + zh}
        return remote(resid, xs.at[w], z_at + 2 * d + e, m, z_at + 2 * zl + c)

    for d, e in ((0, 1), (1, 0), (1, 1)):
        over_z(d, e).start()

    @pl.when(away)
    def _():
        over_z(0, 0).start()

    sq.relay()
    sd.start_away()

    suffix_at = at
    at += 2
    suffix = ((sk_in.at[0], sk), (sv_in.at[0], sv))

    @pl.when(home)
    def _():
        for j, (src, dst) in enumerate(suffix):
            pltpu.make_async_copy(src, dst, lsem.at[5 + j]).start()

    @pl.when(away)
    def _():
        for j, (src, dst) in enumerate(suffix):
            remote(src, dst, suffix_at + j, swap).start()

    def over_y(i, d):
        block = 4 * y + i
        m = {"wide": (2 * lax.rem(y + d, 4) + zl) * 2 + c}
        return remote(xs.at[block], xs.at[block], y_at + 4 * (d - 1) + i, m)

    for i in range(4):
        block = 4 * y + i

        @pl.when(jnp.logical_not(jnp.logical_and(home, 2 * zl + c == i)))
        def _():
            remote(xs.at[block], xs.at[block], z_at + i, sibling).wait_recv()

        for d in range(1, 4):
            over_y(i, d).start()

    pre_at = at
    at += 16
    prefix = ((pk_in, pk), (pv_in, pv))

    def over_x(j, d, e):
        src, dst = prefix[j]
        px, pc = lax.rem(x + d, 4), lax.rem(c + e, 2)
        m = {"narrow": 2 * px + c, "wide": 2 * wc + pc}
        return remote(src.at[2 * px + pc], dst.at[n], pre_at + 8 * j + 2 * d + e, m, pre_at + 8 * j + 4 * zh + d)

    for j in range(2):
        for d in range(4):
            for e in range(2):
                if d or e:
                    over_x(j, d, e).start()

    @pl.when(home)
    def _():
        for j, (src, dst) in enumerate(prefix):
            pltpu.make_async_copy(src.at[n], dst.at[n], lsem.at[7 + j]).start()

    @pl.when(away)
    def _():
        for j in range(2):
            over_x(j, 0, 0).start()

    so.start_home()
    so.start_away()
    su.start_home()
    su.start_away()
    sq.pass_on()
    sd.relay()
    for i in range(4):
        for d in range(1, 4):
            block = 4 * lax.rem(y + 4 - d, 4) + i
            remote(xs.at[block], xs.at[block], y_at + 4 * (d - 1) + i, sibling).wait_recv()

    sq.share()
    total_feats = wide * feats

    @pl.loop(0, tokens // 32)
    def _(i):
        r = pl.ds(pl.multiple_of(i * 32, 32), 32)
        total = xs[0, r, :].astype(F32)
        for m in range(1, wide):
            total = total + xs[m, r, :].astype(F32)
        mean = jnp.sum(total, axis=-1, keepdims=True) * (1.0 / total_feats)
        var = jnp.zeros_like(total)
        for m in range(wide):
            center = xs[m, r, :].astype(F32) - mean
            var = var + center * center
        inv = lax.rsqrt(jnp.sum(var, axis=-1, keepdims=True) * (1.0 / total_feats) + 1e-05)
        for m in range(wide):
            cols = slice(m * feats, (m + 1) * feats)
            normed = (xs[m, r, :].astype(F32) - mean) * inv
            na[r, cols] = (normed * gains[0:1, cols]).astype(BF16)
            nm[r, cols] = (normed * gains[1:2, cols]).astype(BF16)

    so.relay()
    su.relay()
    sd.pass_on()
    sq.complete()

    @pl.loop(0, wq.shape[2] // 256)
    def _(j):
        cols = pl.ds(pl.multiple_of(j * 256, 256), 256)
        weight = wq[:, :, cols].reshape(na.shape[1], 256)
        qkv[:, cols] = jnp.dot(na[...], weight, preferred_element_type=F32).astype(BF16)

    sd.share()

    @pl.loop(0, 4)
    def _(i):
        r = pl.ds(pl.multiple_of(i * 128, 128), 128)
        for h in range(2):
            for t in range(2):
                cols = slice((3 * h + t) * HD, (3 * h + t + 1) * HD)
                v = qkv[r, cols].astype(F32)
                turned = v * cos_t[r, :] + pltpu.roll(v, HD - ROT // 2, 1) * sin_a[r, :] + pltpu.roll(v, ROT // 2, 1) * sin_b[r, :]
                qkv[r, cols] = turned.astype(BF16)

    @pl.when(home)
    def _():
        for j, (src, dst) in enumerate(suffix):
            pltpu.make_async_copy(src, dst, lsem.at[5 + j]).wait()

    @pl.when(away)
    def _():
        for j, (src, dst) in enumerate(suffix):
            remote(src, dst, suffix_at + j, swap).wait_recv()

    for j, (src, dst) in enumerate(prefix):
        for sz in range(2):
            for d in range(4):
                m = 2 * lax.rem(x + 4 - d, 4) + sz
                arrival = remote(dst.at[m], dst.at[m], pre_at, sibling, pre_at + 8 * j + 4 * sz + d)
                if d:
                    arrival.wait_recv()
                else:
                    mine = jnp.logical_and(home, zh == sz)

                    @pl.when(mine)
                    def _():
                        pltpu.make_async_copy(src.at[n], dst.at[n], lsem.at[7 + j]).wait()

                    @pl.when(jnp.logical_not(mine))
                    def _():
                        arrival.wait_recv()

    pre_len = pk.shape[0] * pk.shape[1]
    suf_len = sk.shape[0]
    qc = scores.shape[0]

    def attend(h):
        hc = slice(h * HD, (h + 1) * HD)
        q_cols = slice(3 * h * HD, (3 * h + 1) * HD)
        k_cols = slice((3 * h + 1) * HD, (3 * h + 2) * HD)
        v_cols = slice((3 * h + 2) * HD, (3 * h + 3) * HD)

        @pl.loop(0, tokens // qc)
        def _(i):
            r = pl.ds(pl.multiple_of(i * qc, qc), qc)
            q = qkv[r, q_cols]

            def score(keys):
                return lax.dot_general(q, keys, (((1,), (1,)), ((), ())), preferred_element_type=F32) * scale

            keys = pk[:, :, hc].reshape(pre_len, HD)
            s = score(keys) + bias[0:1, 0:pre_len]
            scores[:, 0:pre_len] = s
            top = jnp.max(s, axis=-1, keepdims=True)
            for b in range(suf_len // 512):
                lo = pre_len + b * 512
                s = score(sk[b * 512 : (b + 1) * 512, hc]) + bias[0:1, lo : lo + 512]
                scores[:, lo : lo + 512] = s
                top = jnp.maximum(top, jnp.max(s, axis=-1, keepdims=True))
            lo = pre_len + suf_len
            s = score(qkv[:, k_cols])
            row = lax.broadcasted_iota(jnp.int32, s.shape, 0) + i * qc
            col = lax.broadcasted_iota(jnp.int32, s.shape, 1)
            s = jnp.where(row >= col, s, NEG)
            scores[:, lo : lo + tokens] = s
            top = jnp.maximum(top, jnp.max(s, axis=-1, keepdims=True))
            den = jnp.zeros((qc, 1), F32)
            for b in range(scores.shape[1] // 512):
                p = jnp.exp(scores[:, b * 512 : (b + 1) * 512] - top)
                den = den + jnp.sum(p, axis=-1, keepdims=True)
                probs[:, b * 512 : (b + 1) * 512] = p.astype(BF16)
            num = jnp.dot(probs[:, 0:pre_len], pv[:, :, hc].reshape(pre_len, HD), preferred_element_type=F32)
            num = num + jnp.dot(probs[:, pre_len:lo], sv[:, hc], preferred_element_type=F32)
            num = num + jnp.dot(probs[:, lo : lo + tokens], qkv[:, v_cols], preferred_element_type=F32)
            attn[r, hc] = (num / den).astype(BF16)

    so.pass_on()
    su.pass_on()
    attend(0)
    attend(1)
    so.share()
    su.share()

    def up_rows(m, fresh):
        k = pl.ds(pl.multiple_of(m * wu.shape[1], wu.shape[1]), wu.shape[1])

        @pl.loop(0, wu.shape[2] // 256)
        def _(j):
            cols = pl.ds(pl.multiple_of(j * 256, 256), 256)
            part = jnp.dot(nm[:, k], wu[m, :, cols], preferred_element_type=F32)
            if fresh:
                acc[:, cols] = part
            else:
                acc[:, cols] += part

    up_rows(su.first, True)
    for m in su.arrivals:
        up_rows(m, False)
    su.complete()
    for m in su.others():
        up_rows(m, False)

    @pl.loop(0, tokens // 64)
    def _(i):
        r = pl.ds(pl.multiple_of(i * 64, 64), 64)
        u = acc[r, :]
        hid[r, :] = (0.5 * u * (1.0 + lax.erf(u * math.sqrt(0.5)))).astype(BF16)

    sd.complete()
    so.complete()

    sum_at = at
    at += 3
    part_at = at
    at += 4
    span = wd.shape[2]

    def terms(m):
        return jnp.dot(hid[...], wd[m], preferred_element_type=F32) + jnp.dot(
            attn[...], wo[m], preferred_element_type=F32
        )

    def to_y(r):
        m = {"wide": (2 * lax.rem(y + 1 + r, 4) + zl) * 2 + c}
        return remote(ry_s.at[r], ry_r.at[r], sum_at + r, m)

    for r in range(3):

        @pl.loop(0, 2)
        def _(j):
            cols = pl.ds(pl.multiple_of(j * span, span), span)
            ry_s[r, :, cols] = terms(2 * lax.rem(y + 1 + r, 4) + j).astype(BF16)

        to_y(r).start()

    @pl.loop(0, 2)
    def _(j):
        cols = pl.ds(pl.multiple_of(j * span, span), span)
        acc[:, cols] = terms(2 * y + j)

    for r in range(3):
        to_y(r).wait_recv()
    spot = 2 * zh + zl

    def to_z(i):
        m = {"narrow": 2 * x + c, "wide": 4 * y + i}
        return remote(rz_s.at[i], rz_r.at[spot], part_at + i, m, part_at + spot)

    for i in range(4):
        cols = slice(i * feats, (i + 1) * feats)

        @pl.loop(0, tokens // 64)
        def _(k):
            r = pl.ds(pl.multiple_of(k * 64, 64), 64)
            total = acc[r, cols]
            for m in range(3):
                total = total + ry_r[m, r, cols].astype(F32)
            rz_s[i, r, :] = total.astype(BF16)

        mine = jnp.logical_and(home, 2 * zl + c == i)

        @pl.when(jnp.logical_not(mine))
        def _():
            to_z(i).start()

        @pl.when(mine)
        def _():
            rz_r[spot] = rz_s[i]

    for i in range(4):

        @pl.when(jnp.logical_not(jnp.logical_and(home, spot == i)))
        def _():
            remote(rz_r.at[i], rz_r.at[i], part_at, sibling, part_at + i).wait_recv()

    @pl.loop(0, tokens // 64)
    def _(i):
        r = pl.ds(pl.multiple_of(i * 64, 64), 64)
        total = rz_r[0, r, :].astype(F32)
        for m in range(1, 4):
            total = total + rz_r[m, r, :].astype(F32)
        out_ref[r, :] = (resid[r, :].astype(F32) + total).astype(BF16)

    tail = out_ref[tokens - 16 : tokens, :].astype(F32)
    last_n[n] = jnp.broadcast_to(tail[15:16, :], (8, feats))
    ln_at = at
    at += 7
    for d in range(1, NN):
        copy = remote(last_n.at[n], last_n.at[n], ln_at + d - 1, {"narrow": lax.rem(n + d, NN)})
        copy.start()
        sends.append(copy)
    for d in range(1, NN):
        src = lax.rem(n + NN - d, NN)
        remote(last_n.at[src], last_n.at[src], ln_at + d - 1, sibling).wait_recv()
    pick_row = lax.broadcasted_iota(jnp.int32, (8, feats), 0)
    eight = last_n[0]
    for m in range(1, NN):
        eight = jnp.where(pick_row == m, last_n[m], eight)
    last_w[w] = eight
    lw_at = at
    at += 15
    for d in range(1, wide):
        copy = remote(last_w.at[w], last_w.at[w], lw_at + d - 1, {"wide": lax.rem(w + d, wide)})
        copy.start()
        sends.append(copy)
    for d in range(1, wide):
        src = lax.rem(w + wide - d, wide)
        remote(last_w.at[src], last_w.at[src], lw_at + d - 1, sibling).wait_recv()
    for m in range(wide):
        last_ref[:, m * feats : (m + 1) * feats] = last_w[m]

    for copy in sends:
        copy.wait_send()
    for name in names:
        spreads[name].finish()
    for d, e in ((0, 1), (1, 0), (1, 1)):
        over_z(d, e).wait_send()
    for i in range(4):
        for d in range(1, 4):
            over_y(i, d).wait_send()
    for j in range(2):
        for d in range(4):
            for e in range(2):
                if d or e:
                    over_x(j, d, e).wait_send()

    @pl.when(away)
    def _():
        over_z(0, 0).wait_send()
        for j, (src, dst) in enumerate(suffix):
            remote(src, dst, suffix_at + j, swap).wait_send()
        for j in range(2):
            over_x(j, 0, 0).wait_send()

    for r in range(3):
        to_y(r).wait_send()
    for i in range(4):

        @pl.when(jnp.logical_not(jnp.logical_and(home, 2 * zl + c == i)))
        def _():
            to_z(i).wait_send()


def layer(rows, wq, wu, wd, wo, pk, pv, sk, sv, owner, gains, cos_t, sin_a, sin_b, bias):
    tokens = rows.shape[0] // NN
    feats = rows.shape[1]
    dim = 2 * NWC * feats
    keys = bias.shape[1]
    qc = 256
    vm = pltpu.VMEM
    anywhere = pl.BlockSpec(memory_space=pl.ANY)
    inside = pl.BlockSpec(memory_space=pltpu.VMEM)
    four = (4, tokens, feats)
    groups = (3, tokens, 4 * feats)
    return pl.pallas_call(
        layer_kernel,
        out_shape=(
            jax.ShapeDtypeStruct((tokens, feats), BF16),
            jax.ShapeDtypeStruct((NN, dim), F32),
        ),
        in_specs=[anywhere] * 9 + [inside] * 6,
        out_specs=(inside, inside),
        scratch_shapes=[
            vm((NN,) + wq.shape, BF16),
            vm((NN,) + wu.shape, BF16),
            vm((NN,) + wd.shape, BF16),
            vm((NN,) + wo.shape, BF16),
            vm(pk.shape, BF16),
            vm(pv.shape, BF16),
            vm(sk.shape[1:], BF16),
            vm(sv.shape[1:], BF16),
            vm((NN, tokens, feats), BF16),
            vm((tokens, feats), BF16),
            vm((2 * NWC, tokens, feats), BF16),
            vm((tokens, dim), BF16),
            vm((tokens, dim), BF16),
            vm((tokens, wq.shape[1]), BF16),
            vm((qc, keys), F32),
            vm((qc, keys), BF16),
            vm((tokens, feats), BF16),
            vm((tokens, wu.shape[1]), F32),
            vm((tokens, wu.shape[1]), BF16),
            vm(groups, BF16),
            vm(groups, BF16),
            vm(four, BF16),
            vm(four, BF16),
            vm((NN, 8, feats), F32),
            vm((2 * NWC, 8, feats), F32),
            pltpu.SemaphoreType.DMA((112,)),
            pltpu.SemaphoreType.DMA((112,)),
            pltpu.SemaphoreType.DMA((9,)),
        ],
        compiler_params=pltpu.CompilerParams(
            collective_id=1, has_side_effects=True, vmem_limit_bytes=VMEM_LIMIT
        ),
    )(rows, wq, wu, wd, wo, pk, pv, sk, sv, owner, gains, cos_t, sin_a, sin_b, bias)


def body(
    token_ids,
    group_ids,
    prefix_lengths,
    cached_lengths,
    embedding,
    ln_gains,
    qkv_weight,
    out_weight,
    up_weight,
    down_weight,
    prefix_keys,
    prefix_values,
    suffix_keys,
    suffix_values,
    final_gain,
    head_weight,
):
    n = lax.axis_index("narrow")
    stretch = token_ids.shape[0]
    all_ids = gather_ids(token_ids)
    vocab_rows = embedding.shape[0]
    local_ids = all_ids - n * vocab_rows
    rows = embedding.at[jnp.clip(local_ids, 0, vocab_rows - 1)].get(mode="promise_in_bounds")
    owner = jnp.broadcast_to((token_ids // vocab_rows)[:, None], (stretch, embedding.shape[1]))

    second = (group_ids == 1)[:, None, None]
    pk = jnp.where(second, prefix_keys[1][None], prefix_keys[0][None])
    pv = jnp.where(second, prefix_values[1][None], prefix_values[0][None])
    me = (2 * (n // 2) + lax.axis_index("wide") % 2)[None]
    group = pick(group_ids, me)
    far = pick(prefix_lengths, group)[0]
    cached = pick(cached_lengths, me)[0]
    places = (far + cached + jnp.arange(stretch, dtype=jnp.int32)).astype(F32)
    half = ROT // 2
    freqs = jnp.power(10000.0, -(jnp.arange(half).astype(F32) * 2.0 / ROT))
    angles = places[:, None] * freqs[None, :]
    cosine, sine = jnp.cos(angles), jnp.sin(angles)
    rest = HD - ROT
    cos_t = jnp.concatenate([cosine, cosine, jnp.ones((stretch, rest), F32)], axis=1)
    sin_a = jnp.concatenate([-sine, jnp.zeros((stretch, HD - half), F32)], axis=1)
    sin_b = jnp.concatenate([jnp.zeros((stretch, half), F32), sine, jnp.zeros((stretch, rest), F32)], axis=1)
    pre = NN * prefix_keys.shape[1]
    ok = jnp.concatenate(
        [
            jnp.arange(pre, dtype=jnp.int32) < far,
            jnp.arange(suffix_keys.shape[1], dtype=jnp.int32) < cached,
            jnp.ones((stretch,), bool),
        ]
    )
    bias = jnp.broadcast_to(jnp.where(ok, 0.0, NEG).astype(F32)[None, :], (8, ok.shape[0]))

    hidden_out, last_values = layer(
        rows,
        qkv_weight,
        up_weight,
        down_weight,
        out_weight,
        pk,
        pv,
        suffix_keys,
        suffix_values,
        owner,
        ln_gains,
        cos_t,
        sin_a,
        sin_b,
        bias,
    )
    last_rms = jnp.sqrt(jnp.mean(last_values * last_values, axis=-1))
    final_rows = layer_norm(last_values, final_gain).astype(BF16)
    logits = jnp.dot(final_rows, head_weight, preferred_element_type=F32)
    max_logit = max_over_all(jnp.max(logits, axis=-1))
    return (hidden_out, last_rms, max_logit)


def solution(mesh):
    return jax.shard_map(
        body,
        mesh=mesh,
        in_specs=(
            P("narrow"),
            P(),
            P(),
            P(),
            P("narrow", "wide"),
            P(),
            P("narrow", "wide"),
            P("wide", "narrow"),
            P("narrow", "wide"),
            P("wide", "narrow"),
            P(None, "narrow", "wide"),
            P(None, "narrow", "wide"),
            P("narrow", None, "wide"),
            P("narrow", None, "wide"),
            P(),
            P(None, ("wide", "narrow")),
        ),
        out_specs=(P("narrow", "wide"), P(), P()),
        check_vma=False,
    )
```
